128 devices in a mesh: row: 8 (over x, core), col: 16 (over z, y).
Axes of the slice: x: 4, y: 4, z: 4, core: 2. Of those that a mesh axis runs over, the one named last changes fastest.
Arguments:
- tokens: bfloat16 [1536, 6144], P('row', 'col'), may hold values from -6 to 6
- out_grad: bfloat16 [1536, 6144], P('row', 'col'), may hold values from -6 to 6
- w_up: bfloat16 [6144, 24576], P('col', 'row'), may hold values from -0.078125 to 0.078125
- w_down: bfloat16 [24576, 6144], P('row', 'col'), may hold values from -0.078125 to 0.078125
- mask_up: int32 [96, 384], P('col', 'row'), may hold values from 0 to 1, as said below
- mask_down: int32 [384, 96], P('row', 'col'), may hold values from 0 to 1, as said below
- acc_up: float32 [6144, 24576], P('col', 'row'), may hold values from -96 to 96
- acc_down: float32 [24576, 6144], P('row', 'col'), may hold values from -96 to 96
Outputs:
- in_grad: bfloat16 [1536, 6144], P('row', 'col')
- new_acc_up: float32 [6144, 24576], P('col', 'row')
- new_acc_down: float32 [24576, 6144], P('row', 'col')
The draws below stay inside these ranges and needn't reach their ends.
Inputs may be any that keep to these rules, and one draw needn't show every extreme that they name: `mask_up`: each entry is 0 (pruned block) or 1 (kept block); the share of kept blocks varies between block rows and block columns. `mask_down`: each entry is 0 (pruned block) or 1 (kept block); the share of kept blocks varies between block rows and block columns.
All inputs are finite; a program needn't handle non-finite values.
Results may differ from the reference program's by a relative error of at most 0.028.
Values may be sent and summed in bfloat16 or wider, within the bound.
No kernel may reach another device: no remote copies, remote signals or barrier semaphores. Data moves between devices by JAX's collectives and lax.ppermute only.
A program may use at most 192 MiB of HBM per device.

```python
import math
import jax
import jax.numpy as jnp
from jax import lax

D = 6144
FF = 24576
BLK = 64
TOKENS = 1536
FEAT_BLOCK = 384
N_COL = 16


def block_pattern(seed_key, rows, cols):
    keys = jax.random.split(seed_key, 3)
    row_level = jax.random.randint(keys[0], (rows, 1), 10, 50)
    col_level = jax.random.randint(keys[1], (1, cols), 10, 50)
    values = jax.random.randint(keys[2], (rows, cols), 0, 100)
    return jnp.where(values < row_level + col_level, 1, 0).astype(jnp.int32)


def draw_mask_up(key, part):
    return block_pattern(jax.random.fold_in(key, 11), D // BLK, FF // BLK)


def draw_mask_down(key, part):
    return block_pattern(jax.random.fold_in(key, 23), FF // BLK, D // BLK)


def block_levels(own_key, extent, cuts, low, high):
    factor_of, own = 1.0, jax.random.fold_in(own_key, 6)
    for position, blocks in cuts:
        steps = jnp.exp(jax.random.uniform(jax.random.fold_in(own, position), (blocks,), jnp.float32, low / len(cuts), high / len(cuts)))
        factor_of = factor_of * jnp.repeat(steps, extent[position] // blocks).reshape([-1 if axis == position else 1 for axis in range(len(extent))])
    return factor_of


def scatter_about(own_key, dims, scale, most, cuts=(), dtype=jnp.bfloat16):
    entries = jax.random.normal(own_key, dims, jnp.float32) * scale
    if len(cuts) > 0:
        entries = block_levels(own_key, dims, cuts, -0.22, 0.18) * entries
    return jnp.clip(entries, min=-most, max=most).astype(dtype)


def setup_inputs(seed: int = 0) -> dict:
    arg_keys = jax.random.split(jax.random.key(seed), 9)
    return {
        "tokens": scatter_about(arg_keys[0], (TOKENS, D), 1.0, 6.0, ((0, 8), (1, 16))),
        "out_grad": scatter_about(arg_keys[1], (TOKENS, D), 1.0, 6.0, ((0, 8), (1, 16))),
        "w_up": scatter_about(arg_keys[2], (D, FF), D ** -0.5, 0.078125, ((0, 16), (1, 8))),
        "w_down": scatter_about(arg_keys[3], (FF, D), D ** -0.5, 0.078125, ((0, 8), (1, 16))),
        "mask_up": draw_mask_up(jax.random.fold_in(arg_keys[8], 71), 0),
        "mask_down": draw_mask_down(jax.random.fold_in(arg_keys[8], 71), 0),
        "acc_up": scatter_about(arg_keys[6], (D, FF), 16.0, 96.0, ((0, 16), (1, 8)), jnp.float32),
        "acc_down": scatter_about(arg_keys[7], (FF, D), 16.0, 96.0, ((0, 8), (1, 16)), jnp.float32),
    }


def spread_mask(mask_grid):
    rows, cols = mask_grid.shape
    full = jnp.broadcast_to(mask_grid[:, None, :, None], (rows, BLK, cols, BLK))
    return full.reshape(rows * BLK, cols * BLK).astype(jnp.bfloat16)

def gelu_parts(value):
    cdf = 0.5 * (1.0 + jax.scipy.special.erf(value / math.sqrt(2.0)))
    pdf = jnp.exp(-0.5 * value * value) / math.sqrt(2.0 * math.pi)
    return (value * cdf, cdf + value * pdf)

def reference(tokens, out_grad, w_up, w_down, mask_up, mask_down, acc_up, acc_down):
    up_eff = w_up * spread_mask(mask_up)
    down_eff = w_down * spread_mask(mask_down)
    pre = jnp.zeros((TOKENS, FF), jnp.float32)
    back = jnp.zeros((TOKENS, FF), jnp.float32)
    for index in range(N_COL):
        lower = index * FEAT_BLOCK
        upper = lower + FEAT_BLOCK
        part_pre = jnp.dot(tokens[:, lower:upper], up_eff[lower:upper, :], preferred_element_type=jnp.float32)
        part_back = jnp.dot(out_grad[:, lower:upper], down_eff[:, lower:upper].T, preferred_element_type=jnp.float32)
        part_pre = lax.optimization_barrier(part_pre.astype(jnp.bfloat16))
        part_back = lax.optimization_barrier(part_back.astype(jnp.bfloat16))
        pre = pre + part_pre.astype(jnp.float32)
        back = back + part_back.astype(jnp.float32)
    act_value, act_slope = gelu_parts(pre)
    hidden = act_value.astype(jnp.bfloat16)
    pre_grad = (back * act_slope).astype(jnp.bfloat16)
    grad_up = jnp.dot(tokens.T, pre_grad, preferred_element_type=jnp.float32)
    new_acc_up = acc_up + spread_mask(mask_up).astype(jnp.float32) * grad_up
    grad_down = jnp.dot(hidden.T, out_grad, preferred_element_type=jnp.float32)
    new_acc_down = acc_down + spread_mask(mask_down).astype(jnp.float32) * grad_down
    in_grad = jnp.dot(pre_grad, up_eff.T, preferred_element_type=jnp.float32).astype(jnp.bfloat16)
    return (in_grad, new_acc_up, new_acc_down)
```

```python
import math

import jax
import jax.numpy as jnp
from jax import lax
from jax.experimental import pallas as pl
from jax.experimental.pallas import tpu as pltpu
from jax.sharding import PartitionSpec as P

AXES = ("row", "col")
NT = (((1,), (1,)), ((), ()))
TN = (((0,), (0,)), ((), ()))
NN = (((1,), (0,)), ((), ()))
BF16 = jnp.bfloat16
F32 = jnp.float32
VMEM = 48 * 1024 * 1024
KB = 384
SUB = 192
SEQ = 1536
ORDER = (2, 1, 3, 0)


def ident(x, core, z, y):
    return ((x % 4 * 2 + core) * 4 + z % 4) * 4 + y % 4


def table(target):
    pairs = []
    for x in range(4):
        for core in range(2):
            for z in range(4):
                for y in range(4):
                    there = target(x, core, z, y)
                    if there is not None:
                        pairs.append((ident(x, core, z, y), ident(*there)))
    return pairs


def merge_to(step, role, x, core, z, y):
    return (x, role, z, y + step) if role == 0 else (x, role, z + step, y)


def reduce_to(step, role, x, core, z, y):
    return (x, role, z + step, y) if role == 0 else (x, role, z, y + step)


def send(value, target):
    return lax.ppermute(value, AXES, table(target))


def send_weights(step, own):
    return lambda x, core, z, y: merge_to(step, core if own else 1 - core, x, core, z, y)


def send_reduce(step, own):
    def target(x, core, z, y):
        tx, _, tz, ty = reduce_to(step, core, x, core, z, y)
        return (tx, core if own else 1 - core, tz, ty)

    return target


def send_gather(step, own):
    return lambda x, core, z, y: reduce_to(step, core if own else 1 - core, x, core, z, y)


def send_grads(step, own):
    def target(x, core, z, y):
        tx, _, tz, ty = merge_to(step, core, x, core, z, y)
        return (tx, core if own else 1 - core, tz, ty)

    return target


def call(body, grid, in_specs, out_specs, out_shape, flops, moved, aliases={}, scratch=()):
    return pl.pallas_call(
        body,
        grid_spec=pltpu.PrefetchScalarGridSpec(
            num_scalar_prefetch=1,
            grid=grid,
            in_specs=in_specs,
            out_specs=out_specs,
            scratch_shapes=list(scratch),
        ),
        out_shape=out_shape,
        input_output_aliases=aliases,
        compiler_params=pltpu.CompilerParams(vmem_limit_bytes=VMEM),
        cost_estimate=pl.CostEstimate(flops=flops, bytes_accessed=moved, transcendentals=0),
    )


def whole(shape):
    return pl.BlockSpec(shape, lambda i, s: (0,) * len(shape))


def one_hot(rows, cols, hit):
    r = lax.broadcasted_iota(jnp.int32, (rows, cols), 0)
    q = lax.broadcasted_iota(jnp.int32, (rows, cols), 1)
    return jnp.where(hit(r, q), 1.0, 0.0).astype(F32)


def mm(left, right, dims):
    return lax.dot_general(left, right, dims, preferred_element_type=F32)


def mod4(value):
    return lax.rem(value + 8, 4)


def up_mask_rows(mask, y, z, step):
    blk = mask.shape[0]
    wide = mm(mask.astype(F32), one_hot(blk, KB, lambda r, q: q // 64 == r), TN)
    yy = mod4(y + step)
    pick = one_hot(12, 48, lambda r, q: q == (yy * 4 + mod4(z + r // 3)) * 3 + lax.rem(r, 3))
    return mm(pick, wide, NN)


def down_mask_rows(mask, y, z, step):
    blk = mask.shape[1]
    wide = mm(mask.astype(F32), one_hot(blk, KB, lambda r, q: q // 64 == r), NN)
    zz = mod4(z + step)
    pick = one_hot(12, 48, lambda r, q: q == (mod4(y + r // 3) * 4 + zz) * 3 + lax.rem(r, 3))
    return mm(pick, wide, NN)


def prepare(step, where, w_up, w_down4, mask_up, mask_down):
    def body(s, up_ref, down_ref, mu_ref, md_ref, own_ref, oth_ref, turned):
        y, z, core = s[0], s[1], s[2]
        turned[...] = up_ref[...].T
        mu = up_mask_rows(mu_ref[...], y, z, step).astype(BF16)
        md = down_mask_rows(md_ref[...], y, z, step).astype(BF16)

        def put(up_out, down_out):
            for f in range(4):
                at = pl.multiple_of(mod4(z + f) * SUB, SUB)
                part = turned[pl.ds(at, SUB), :].reshape(3, 64, KB) * mu[f * 3 : f * 3 + 3][:, None, :]
                up_out[f * SUB : (f + 1) * SUB, :] = part.reshape(SUB, KB)
                part = down_ref[mod4(y + f), 0].reshape(3, 64, KB) * md[f * 3 : f * 3 + 3][:, None, :]
                down_out[f * SUB : (f + 1) * SUB, :] = part.reshape(SUB, KB)

        @pl.when(core == 0)
        def _():
            put(own_ref, oth_ref)

        @pl.when(core != 0)
        def _():
            put(oth_ref, own_ref)

    shape = jax.ShapeDtypeStruct((4 * SUB, KB), BF16)
    return call(
        body,
        (1,),
        [
            pl.BlockSpec((KB, 4 * SUB), lambda i, s: (0, mod4(s[0] + step))),
            pl.BlockSpec((4, 1, SUB, KB), lambda i, s: (0, mod4(s[1] + step), 0, 0)),
            whole(mask_up.shape),
            whole(mask_down.shape),
        ],
        [whole(shape.shape)] * 2,
        [shape] * 2,
        10**7,
        2_400_000,
        scratch=[pltpu.VMEM((4 * SUB, KB), BF16)],
    )(where, w_up, w_down4, mask_up, mask_down)


def forward(step, where, weights, acts):
    def body(s, *refs):
        w, a, o = refs[:8], refs[8:12], refs[12:]
        left = jnp.concatenate(
            [jnp.concatenate([w[e * 2 + h][...] for e in range(4)], axis=1) for h in range(2)], axis=0
        )
        for d in range(4):
            right = jnp.concatenate([a[d][e] for e in range(4)], axis=1)
            total = mm(left, right, NT).astype(BF16)
            o[0][:, d * KB : (d + 1) * KB] = total[:SUB]
            o[1][:, d * KB : (d + 1) * KB] = total[SUB:]

    shape = jax.ShapeDtypeStruct((SUB, SEQ), BF16)
    return call(
        body,
        (1,),
        [pl.BlockSpec((SUB, KB), lambda i, s: (step, 0))] * 8 + [whole((4, KB, KB))] * 4,
        [whole(shape.shape)] * 2,
        [shape] * 2,
        2 * 384 * 1536 * 1536,
        7_100_000,
    )(where, *[weights[e][h] for e in range(4) for h in range(2)], *acts)


def gelu_parts(value):
    cdf = 0.5 * (1.0 + lax.erf(value / math.sqrt(2.0)))
    pdf = jnp.exp(-0.5 * value * value) / math.sqrt(2.0 * math.pi)
    return (value * cdf, cdf + value * pdf)


def activate(where, own, oth):
    def body(s, *refs):
        ins, (own_out, oth_out) = refs[:8], refs[8:]
        first = sum(r[...].astype(F32) for r in ins[:4])
        second = sum(r[...].astype(F32) for r in ins[4:])

        def put(pre, back, grad_out, hid_out):
            act, slope = gelu_parts(pre)
            hid_out[...] = act.astype(BF16)
            grad_out[...] = (back * slope).astype(BF16)

        @pl.when(s[2] == 0)
        def _():
            put(first, second, own_out, oth_out)

        @pl.when(s[2] != 0)
        def _():
            put(second, first, oth_out, own_out)

    shape = jax.ShapeDtypeStruct((SUB, SEQ), BF16)
    block = pl.BlockSpec((SUB // 4, SEQ), lambda i, s: (i, 0))
    return call(body, (4,), [block] * 8, [block] * 2, [shape] * 2, 10**7, 6_000_000)(where, *own, *oth)


def weight_grads(step, where, cots, acts):
    def body(s, *refs):
        c, a, o = refs[:8], refs[8:12], refs[12:]
        right = jnp.concatenate([a[d][0] for d in range(4)], axis=0)
        for f in range(4):
            for h in range(2):
                o[h][f] = mm(c[f * 2 + h][...], right, NN).astype(BF16)

    shape = jax.ShapeDtypeStruct((4, SUB, KB), BF16)
    return call(
        body,
        (1,),
        [whole((SUB, SEQ))] * 8 + [pl.BlockSpec((1, KB, KB), lambda i, s: (step, 0, 0))] * 4,
        [whole(shape.shape)] * 2,
        [shape] * 2,
        2 * 384 * 1536 * 1536,
        7_100_000,
    )(where, *[cots[f][h] for f in range(4) for h in range(2)], *acts)


def input_grads(step, where, cots, weights):
    def body(s, *refs):
        c, w, o = refs[:8], refs[8:16], refs[16:]

        @pl.when(s[2] == 0)
        def _():
            left = jnp.concatenate([c[f * 2 + h][...] for h in range(2) for f in range(4)], axis=0)
            for e in range(4):
                right = jnp.concatenate([w[e * 2 + h][...] for h in range(2)], axis=0)
                total = mm(left, right, TN).astype(BF16)
                o[0][:, e * KB : (e + 1) * KB] = total[:SUB]
                o[1][:, e * KB : (e + 1) * KB] = total[SUB:]

        @pl.when(s[2] != 0)
        def _():
            o[0][...] = jnp.zeros_like(o[0])
            o[1][...] = jnp.zeros_like(o[1])

    shape = jax.ShapeDtypeStruct((SUB, SEQ), BF16)
    return call(
        body,
        (1,),
        [pl.BlockSpec((SUB, KB), lambda i, s: (0, step))] * 8 + [whole((4 * SUB, KB))] * 8,
        [whole(shape.shape)] * 2,
        [shape] * 2,
        2 * 384 * 1536 * 1536,
        7_100_000,
    )(
        where,
        *[cots[f][h] for f in range(4) for h in range(2)],
        *[weights[e][h] for e in range(4) for h in range(2)],
    )


def accumulate(step, where, acc_up, acc_down4, own, oth, mask_up, mask_down, before):
    def body(s, up_ref, down_ref, own_ref, oth_ref, mu_ref, md_ref, *rest):
        up_out, down_out, wide = rest[-3:]
        y, z, core = s[0], s[1], s[2]
        mu = up_mask_rows(mu_ref[...], y, z, step)
        md = down_mask_rows(md_ref[...], y, z, step)

        def put(up_grad, down_grad):
            for f in range(4):
                at = pl.multiple_of(mod4(z + f) * SUB, SUB)
                part = up_grad[f].astype(F32).reshape(3, 64, KB) * mu[f * 3 : f * 3 + 3][:, None, :]
                wide[pl.ds(at, SUB), :] = part.reshape(SUB, KB)
                part = down_grad[f].astype(F32).reshape(3, 64, KB) * md[f * 3 : f * 3 + 3][:, None, :]
                down_out[mod4(y + f), 0] = down_ref[mod4(y + f), 0] + part.reshape(SUB, KB)

        @pl.when(core == 0)
        def _():
            put(own_ref, oth_ref)

        @pl.when(core != 0)
        def _():
            put(oth_ref, own_ref)

        up_out[...] = up_ref[...] + wide[...].T

    up_block = pl.BlockSpec((KB, 4 * SUB), lambda i, s: (0, mod4(s[0] + step)))
    down_block = pl.BlockSpec((4, 1, SUB, KB), lambda i, s: (0, mod4(s[1] + step), 0, 0))
    kept = list(before)
    return call(
        body,
        (1,),
        [up_block, down_block, whole((4, SUB, KB)), whole((4, SUB, KB)), whole(mask_up.shape), whole(mask_down.shape)]
        + [pl.BlockSpec(memory_space=pl.ANY)] * len(kept),
        [up_block, down_block],
        [jax.ShapeDtypeStruct(acc_up.shape, F32), jax.ShapeDtypeStruct(acc_down4.shape, F32)],
        10**7,
        6_000_000,
        aliases={7: 0, 8: 1} if kept else {},
        scratch=[pltpu.VMEM((4 * SUB, KB), F32)],
    )(where, acc_up, acc_down4, own, oth, mask_up, mask_down, *kept)


def local(tokens, out_grad, w_up, w_down, mask_up, mask_down, acc_up, acc_down):
    row, col = lax.axis_index("row"), lax.axis_index("col")
    core, z, y = lax.rem(row, 2), lax.div(col, 4), lax.rem(col, 4)
    where = jnp.stack([y, z, core]).astype(jnp.int32)
    first = core == 0
    w_down4 = w_down.reshape(4, 4, SUB, KB)
    acc_down4 = acc_down.reshape(4, 4, SUB, KB)

    away = send(jnp.where(first, out_grad, tokens), lambda x, core, z, y: (x, 1 - core, z, y))
    mine = jnp.where(first, tokens, out_grad)
    block = jnp.concatenate([jnp.where(first, mine, away), jnp.where(first, away, mine)], axis=0)
    block_far = send(block, lambda x, core, z, y: (x + 2, core, z, y))
    near, far = [block, None, None, None], [block_far, None, None, None]
    for step in (1, 3, 2):
        near[-step % 4] = send(block, lambda x, core, z, y: merge_to(step, core, x, core, z, y))
    acts = [jnp.stack(near), None, None, None]
    for step in (1, 3):
        acts[-step % 4] = send(acts[0], lambda x, core, z, y: (x + step, core, z, y))
    for step in (1, 3, 2):
        far[-step % 4] = send(block_far, lambda x, core, z, y: merge_to(step, core, x, core, z, y))
    acts[2] = jnp.stack(far)

    weights = [None] * 4
    for step in ORDER:
        own, oth = prepare(step, where, w_up, w_down4, mask_up, mask_down)
        if step != 0:
            own = send(own, send_weights(step, True))
        oth = send(oth, send_weights(step, False))
        weights[-step % 4] = (own, oth)

    own_parts, oth_parts = [], []
    for step in ORDER:
        own, oth = forward(step, where, weights, acts)
        if step != 0:
            own = send(own, send_reduce(step, True))
        own_parts.append(own)
        oth_parts.append(send(oth, send_reduce(step, False)))

    own, oth = activate(where, own_parts, oth_parts)
    cots = [None] * 4
    for step in ORDER:
        cots[-step % 4] = (
            send(own, send_gather(step, True)) if step != 0 else own,
            send(oth, send_gather(step, False)),
        )

    sums = []
    for step in ORDER:
        low, high = input_grads(step, where, cots, weights)
        if step != 0:
            low = send(low, lambda x, core, z, y: (x + step, 0, z, y) if core == 0 else None)
        high = send(high, lambda x, core, z, y: (x + step, 1, z, y) if core == 0 else None)
        sums += [low, high]

    grads = [None] * 4
    for step in ORDER:
        own, oth = weight_grads(step, where, cots, acts)
        if step != 0:
            own = send(own, send_grads(step, True))
        oth = send(oth, send_grads(step, False))
        grads[-step % 4] = (own, oth)

    part = sum(s.astype(F32) for s in sums).astype(BF16)
    pieces = [part[:, :KB]]
    for step in (1, 2, 3):
        pieces.append(send(part[:, step * KB : (step + 1) * KB], lambda x, core, z, y: (x, core, z, y + step)))
    in_grad = sum(p.astype(F32) for p in pieces).astype(BF16)

    done = ()
    for step in (0, 2, 3, 1):
        done = accumulate(step, where, acc_up, acc_down4, *grads[step], mask_up, mask_down, done)
    return (in_grad, done[0], done[1].reshape(acc_down.shape))


def solution(mesh):
    placed = (
        P("row", "col"),
        P("row", "col"),
        P("col", "row"),
        P("row", "col"),
        P("col", "row"),
        P("row", "col"),
        P("col", "row"),
        P("row", "col"),
    )
    return jax.shard_map(
        local,
        mesh=mesh,
        in_specs=placed,
        out_specs=(P("row", "col"), P("col", "row"), P("row", "col")),
        check_vma=False,
    )
```

```python
import math

import jax
import jax.numpy as jnp
from jax import lax
from jax.experimental import pallas as pl
from jax.experimental.pallas import tpu as pltpu
from jax.sharding import PartitionSpec as P

AXES = ("row", "col")
NT = (((1,), (1,)), ((), ()))
TN = (((0,), (0,)), ((), ()))
NN = (((1,), (0,)), ((), ()))
BF16 = jnp.bfloat16
F32 = jnp.float32
SCOPED = 20 * 1024 * 1024
KB = 384
SUB = 192
SEQ = 1536
ORDER = (2, 1, 3, 0)
PLAN = (("w", 0), ("w", 3), ("w", 1), ("i", 2), ("w", 2), ("i", 1), ("i", 3))


def ident(x, core, z, y):
    return ((x % 4 * 2 + core) * 4 + z % 4) * 4 + y % 4


def table(target):
    pairs = []
    for x in range(4):
        for core in range(2):
            for z in range(4):
                for y in range(4):
                    there = target(x, core, z, y)
                    if there is not None:
                        pairs.append((ident(x, core, z, y), ident(*there)))
    return pairs


def merge_to(step, role, x, core, z, y):
    return (x, role, z, y + step) if role == 0 else (x, role, z + step, y)


def reduce_to(step, role, x, core, z, y):
    return (x, role, z + step, y) if role == 0 else (x, role, z, y + step)


def send(name, value, target):
    with jax.named_scope(name):
        return lax.ppermute(value, AXES, table(target))


def send_weights(step, own):
    return lambda x, core, z, y: merge_to(step, core if own else 1 - core, x, core, z, y)


def send_reduce(step, own):
    def target(x, core, z, y):
        tx, _, tz, ty = reduce_to(step, core, x, core, z, y)
        return (tx, core if own else 1 - core, tz, ty)

    return target


def send_gather(step, own):
    return lambda x, core, z, y: reduce_to(step, core if own else 1 - core, x, core, z, y)


def send_grads(step, own):
    def target(x, core, z, y):
        tx, _, tz, ty = merge_to(step, core, x, core, z, y)
        return (tx, core if own else 1 - core, tz, ty)

    return target


SCALE = 5


def cost(flops, moved):
    return pl.CostEstimate(flops=flops // SCALE, bytes_accessed=moved // SCALE, transcendentals=0)


def call(name, body, grid, in_specs, out_specs, out_shape, flops, moved, aliases={}, scratch=()):
    return pl.pallas_call(
        body,
        name=name,
        grid_spec=pltpu.PrefetchScalarGridSpec(
            num_scalar_prefetch=1,
            grid=grid,
            in_specs=in_specs,
            out_specs=out_specs,
            scratch_shapes=list(scratch),
        ),
        out_shape=out_shape,
        input_output_aliases=aliases,
        compiler_params=pltpu.CompilerParams(vmem_limit_bytes=SCOPED),
        cost_estimate=cost(flops, moved),
    )


def mask_block(step):
    return pl.BlockSpec((1, 12, KB), lambda i, s: (step, 0, 0))


def after(value, *earlier):
    return lax.optimization_barrier((value, *earlier))[0]


def whole(shape):
    return pl.BlockSpec(shape, lambda i, s: (0,) * len(shape))


def one_hot(rows, cols, hit):
    r = lax.broadcasted_iota(jnp.int32, (rows, cols), 0)
    q = lax.broadcasted_iota(jnp.int32, (rows, cols), 1)
    return jnp.where(hit(r, q), 1.0, 0.0).astype(F32)


def mm(left, right, dims):
    return lax.dot_general(left, right, dims, preferred_element_type=F32)


def mod4(value):
    return lax.rem(value + 8, 4)


def spread_masks(where, mask_up, mask_down):
    def body(s, mu_ref, md_ref, up_out, down_out):
        y, z = s[0], s[1]
        wide_up = mm(mu_ref[...].astype(F32), one_hot(6, KB, lambda r, q: q // 64 == r), TN)
        wide_down = mm(md_ref[...].astype(F32), one_hot(6, KB, lambda r, q: q // 64 == r), NN)
        for step in range(4):
            pick = one_hot(
                12, 48, lambda r, q: q == (mod4(y + step) * 4 + mod4(z + r // 3)) * 3 + lax.rem(r, 3)
            )
            up_out[step] = mm(pick, wide_up, NN)
            pick = one_hot(
                12, 48, lambda r, q: q == (mod4(y + r // 3) * 4 + mod4(z + step)) * 3 + lax.rem(r, 3)
            )
            down_out[step] = mm(pick, wide_down, NN)

    shape = jax.ShapeDtypeStruct((4, 12, KB), F32)
    return resident("spread_masks", body, [shape] * 2, 10**6, 100_000)(where, mask_up, mask_down)


def prepare(step, where, w_up, w_down4, mask_up, mask_down):
    def body(s, up_ref, down_ref, mu_ref, md_ref, own_ref, oth_ref, turned):
        y, z, core = s[0], s[1], s[2]
        turned[...] = up_ref[...].T
        mu = mu_ref[0].astype(BF16)
        md = md_ref[0].astype(BF16)

        def put(up_out, down_out):
            for f in range(4):
                at = pl.multiple_of(mod4(z + f) * SUB, SUB)
                part = turned[pl.ds(at, SUB), :].reshape(3, 64, KB) * mu[f * 3 : f * 3 + 3][:, None, :]
                up_out[f * SUB : (f + 1) * SUB, :] = part.reshape(SUB, KB)
                part = down_ref[mod4(y + f), 0].reshape(3, 64, KB) * md[f * 3 : f * 3 + 3][:, None, :]
                down_out[f * SUB : (f + 1) * SUB, :] = part.reshape(SUB, KB)

        @pl.when(core == 0)
        def _():
            put(own_ref, oth_ref)

        @pl.when(core != 0)
        def _():
            put(oth_ref, own_ref)

    own_shape = jax.ShapeDtypeStruct((4 * SUB + KB, KB), BF16)
    oth_shape = jax.ShapeDtypeStruct((4 * SUB, KB), BF16)
    return call(
        f"prepare{step}",
        body,
        (1,),
        [
            pl.BlockSpec((KB, 4 * SUB), lambda i, s: (0, mod4(s[0] + step))),
            pl.BlockSpec((4, 1, SUB, KB), lambda i, s: (0, mod4(s[1] + step), 0, 0)),
            mask_block(step),
            mask_block(step),
        ],
        [whole(own_shape.shape), whole(oth_shape.shape)],
        [own_shape, oth_shape],
        10**7,
        2_400_000,
        scratch=[pltpu.VMEM((4 * SUB, KB), BF16)],
    )(where, w_up, w_down4, mask_up, mask_down)


def resident(name, body, out_shape, flops, moved, aliases={}):
    def make(where, *args):
        return pl.pallas_call(
            body,
            name=name,
            in_specs=[pl.BlockSpec(memory_space=pltpu.SMEM)] + [pl.BlockSpec(memory_space=pltpu.VMEM)] * len(args),
            out_specs=[pl.BlockSpec(memory_space=pltpu.VMEM)] * len(out_shape),
            out_shape=out_shape,
            input_output_aliases=aliases,
            compiler_params=pltpu.CompilerParams(vmem_limit_bytes=SCOPED),
            cost_estimate=cost(flops, moved),
        )(where, *args)

    return make


MATMUL = 2 * 384 * 1536 * 1536


def act_block(acts, weights, d, e):
    return weights[e * 2][4 * SUB :, :] if d == 2 else acts[d if d < 2 else 2][e]


def add_rows(where, buffers, rows):
    def body(s, *refs):
        for out in refs[5:]:
            out[4 * SUB :, :] = refs[4][...]

    shape = jax.ShapeDtypeStruct(buffers[0].shape, BF16)
    return resident("add_rows", body, [shape] * 4, 10**6, 1_000_000, {i + 1: i for i in range(4)})(where, *buffers, rows)


def flat(weights):
    return [weights[e][h] for e in range(4) for h in range(2)]


def forward(step, where, weights, acts):
    def body(s, *refs):
        w, a, o = refs[:8], refs[8:11], refs[11:]
        rows = slice(step * SUB, (step + 1) * SUB)
        left = jnp.concatenate(
            [jnp.concatenate([w[e * 2 + h][rows, :] for e in range(4)], axis=1) for h in range(2)], axis=0
        )
        for d in (0, 2):
            right = jnp.concatenate(
                [jnp.concatenate([act_block(a, w, dd, e) for e in range(4)], axis=1) for dd in (d, d + 1)], axis=0
            )
            total = mm(left, right, NT).astype(BF16)
            o[0][:, d * KB : (d + 2) * KB] = total[:SUB]
            o[1][:, d * KB : (d + 2) * KB] = total[SUB:]

    shape = jax.ShapeDtypeStruct((SUB, SEQ), BF16)
    return resident(f"partial{step}", body, [shape] * 2, MATMUL, 7_100_000)(where, *flat(weights), *acts)


def join(name, where, ours, theirs, at=0):
    def body(s, a, b, out):
        rows = slice(at, at + b.shape[0])
        out[rows, :] = (a[rows, :].astype(F32) + b[...].astype(F32)).astype(BF16)

    shape = jax.ShapeDtypeStruct(ours.shape, BF16)
    return resident(name, body, [shape], 10**6, 2_000_000, {1: 0})(where, ours, theirs)[0]


def gelu_parts(value):
    cdf = 0.5 * (1.0 + lax.erf(value / math.sqrt(2.0)))
    pdf = jnp.exp(-0.5 * value * value) / math.sqrt(2.0 * math.pi)
    return (value * cdf, cdf + value * pdf)


def activate(where, own, oth):
    def body(s, *refs):
        ins, (own_out, oth_out) = refs[:6], refs[6:]

        def put(rows, first, second, grad_out, hid_out):
            pre = sum(r[rows, :].astype(F32) for r in first)
            back = sum(r[rows, :].astype(F32) for r in second)
            act, slope = gelu_parts(pre)
            hid_out[rows, :] = act.astype(BF16)
            grad_out[rows, :] = (back * slope).astype(BF16)

        @pl.loop(0, SUB // 16)
        def _(i):
            rows = pl.ds(pl.multiple_of(i * 16, 16), 16)

            @pl.when(s[2] == 0)
            def _():
                put(rows, ins[:3], ins[3:], own_out, oth_out)

            @pl.when(s[2] != 0)
            def _():
                put(rows, ins[3:], ins[:3], oth_out, own_out)

    shape = jax.ShapeDtypeStruct((SUB, SEQ), BF16)
    return resident("activate", body, [shape] * 2, 10**7, 6_000_000)(where, *own, *oth)


def weight_grads(step, where, cots, weights, acts, before):
    def body(s, *refs):
        c, w, a, o = refs[:2], refs[2:10], refs[10:13], refs[-8:]
        left = jnp.concatenate([c[0][...], c[1][...]], axis=0)
        for e in (0, 2):
            right = jnp.concatenate(
                [jnp.concatenate([act_block(a, w, d, ee) for ee in (e, e + 1)], axis=1) for d in range(4)], axis=0
            )
            total = mm(left, right, NN).astype(BF16)
            for k in range(2):
                for h in range(2):
                    o[(e + k) * 2 + h][step] = total[h * SUB : (h + 1) * SUB, k * KB : (k + 1) * KB]

    shape = jax.ShapeDtypeStruct((4, SUB, KB), BF16)
    return resident(
        f"weight_grads{step}", body, [shape] * 8, MATMUL, 7_100_000, {14 + i: i for i in range(8)} if before else {}
    )(where, *cots, *flat(weights), *acts, *before)


def input_grads(step, where, cots, weights):
    def body(s, *refs):
        c, w, o = refs[:8], refs[8:16], refs[16:]

        @pl.when(s[2] == 0)
        def _():
            left = jnp.concatenate(
                [c[f * 2 + h][:, step * KB : (step + 1) * KB] for h in range(2) for f in range(4)], axis=0
            )
            for e in (0, 2):
                right = jnp.concatenate(
                    [
                        jnp.concatenate([w[ee * 2 + h][: 4 * SUB, :] for h in range(2)], axis=0)
                        for ee in (e, e + 1)
                    ],
                    axis=1,
                )
                total = mm(left, right, TN).astype(BF16)
                for i in range(len(o)):
                    o[i][:, e * KB : (e + 2) * KB] = total[i * rows : (i + 1) * rows]

        @pl.when(s[2] != 0)
        def _():
            for out in o:
                out[...] = jnp.zeros_like(out)

    rows = SUB if step == 2 else 2 * SUB
    shape = jax.ShapeDtypeStruct((rows, SEQ), BF16)
    return resident(f"input_grads{step}", body, [shape] * (2 * SUB // rows), MATMUL, 7_100_000)(
        where, *[cots[f][h] for f in range(4) for h in range(2)], *flat(weights)
    )


def accumulate(step, where, acc_up, acc_down4, own, oth, mask_up, mask_down, before):
    def body(s, up_ref, down_ref, own_ref, oth_ref, mu_ref, md_ref, *rest):
        up_out, down_out, wide = rest[-3:]
        y, z, core = s[0], s[1], s[2]
        mu = mu_ref[0].astype(BF16)
        md = md_ref[0]

        def put(up_grad, down_grad):
            for f in range(4):
                to = pl.multiple_of(mod4(z + f) * SUB, SUB)
                part = up_grad[f].reshape(3, 64, 128) * mu[f * 3 : f * 3 + 3][:, None, :]
                wide[pl.ds(to, SUB), :] = part.reshape(SUB, 128)
                part = down_grad[f].astype(F32).reshape(3, 64, 128) * md[f * 3 : f * 3 + 3][:, None, :]
                down_out[mod4(y + f), 0] = down_ref[mod4(y + f), 0] + part.reshape(SUB, 128)

        @pl.when(core == 0)
        def _():
            put(own_ref, oth_ref)

        @pl.when(core != 0)
        def _():
            put(oth_ref, own_ref)

        up_out[...] = up_ref[...] + wide[...].T.astype(F32)

    up_block = pl.BlockSpec((128, 4 * SUB), lambda i, s: (i, mod4(s[0] + step)))
    down_block = pl.BlockSpec((4, 1, SUB, 128), lambda i, s: (0, mod4(s[1] + step), 0, i))
    mask_block = pl.BlockSpec((1, 12, 128), lambda i, s: (step, 0, i))
    grad_block = pl.BlockSpec((4, SUB, 128), lambda i, s: (0, 0, i))
    kept = list(before)
    return call(
        f"accumulate{step}",
        body,
        (3,),
        [up_block, down_block, grad_block, grad_block, mask_block, mask_block]
        + [pl.BlockSpec(memory_space=pl.ANY)] * len(kept),
        [up_block, down_block],
        [jax.ShapeDtypeStruct(acc_up.shape, F32), jax.ShapeDtypeStruct(acc_down4.shape, F32)],
        10**7,
        6_000_000,
        aliases={7: 0, 8: 1} if kept else {},
        scratch=[pltpu.VMEM((4 * SUB, 128), BF16)],
    )(where, acc_up, acc_down4, own, oth, mask_up, mask_down, *kept)


def local(tokens, out_grad, w_up, w_down, mask_up, mask_down, acc_up, acc_down):
    row, col = lax.axis_index("row"), lax.axis_index("col")
    core, z, y = lax.rem(row, 2), lax.div(col, 4), lax.rem(col, 4)
    where = jnp.stack([y, z, core]).astype(jnp.int32)
    first = core == 0
    w_down4 = w_down.reshape(4, 4, SUB, KB)
    acc_down4 = acc_down.reshape(4, 4, SUB, KB)

    away = send("swap", jnp.where(first, out_grad, tokens), lambda x, core, z, y: (x, 1 - core, z, y))
    mine = jnp.where(first, tokens, out_grad)
    masks = spread_masks(where, mask_up, mask_down)
    owns, oths = [None] * 4, [None] * 4
    for step in ORDER:
        owns[step], oths[step] = prepare(step, where, w_up, w_down4, *masks)
    block = jnp.concatenate([jnp.where(first, mine, away), jnp.where(first, away, mine)], axis=0)
    near = [block, None, None, None]
    for step in (1, 3, 2):
        near[-step % 4] = send(f"near{step}", block, lambda x, core, z, y: merge_to(step, core, x, core, z, y))
    block_far = send("opposite", block, lambda x, core, z, y: (x + 2, core, z, y))
    *near, block_far = lax.optimization_barrier((*near, block_far))
    acts = [jnp.stack(near), None, None]
    for step in (1, 3):
        acts[(-step % 4 + 1) // 2] = send(f"tokens{step}", acts[0], lambda x, core, z, y: (x + step, core, z, y))

    weights = [[None, None] for _ in range(4)]
    for step in ORDER:
        oth = oths[step] if step == 2 else after(oths[step], block_far)
        weights[-step % 4][1] = send(f"w_oth{step}", oth, send_weights(step, False))
    owns = add_rows(where, owns, block_far)
    for step in ORDER:
        own = owns[step]
        weights[-step % 4][0] = send(f"w_own{step}", own, send_weights(step, True)) if step != 0 else own

    parts, turn = {}, where
    for step in ORDER:
        parts[step] = forward(step, turn, weights, acts)
        turn = after(where, parts[step][1])

    def to_sum(step, value, own):
        return send(f"r{step}_{int(own)}", value, send_reduce(step, own))

    half_own, half_oth = to_sum(1, parts[2][0], True), to_sum(3, parts[2][1], True)
    oth_parts = [to_sum(1, parts[1][1], False)]
    own_parts = [to_sum(3, parts[3][0], True)]
    own_parts.append(to_sum(1, join("join_own", where, parts[1][0], half_own), True))
    oth_parts.append(to_sum(3, join("join_oth", where, parts[3][1], half_oth), False))
    own_parts.append(parts[0][0])
    oth_parts.append(to_sum(0, parts[0][1], False))

    own, oth = activate(where, own_parts, oth_parts)

    def to_all(step, value, is_own):
        return send(f"g{step}_{int(is_own)}", value, send_gather(step, is_own))

    left_own, right_oth = to_all(1, own, True), to_all(3, oth, False)
    cots = [
        (own, to_all(0, oth, False)),
        (to_all(3, own, True), right_oth),
        (to_all(1, left_own, True), to_all(3, right_oth, True)),
        (left_own, to_all(1, oth, False)),
    ]

    messages, totals, turn = (), {}, where
    for kind, step in PLAN:
        if kind == "w":
            messages = weight_grads(step, turn, cots[step], weights, acts, messages)
            turn = after(where, messages[0])
        else:
            totals[step] = input_grads(step, turn, cots, weights)
            turn = after(where, totals[step][0])

    def to_x(step, value):
        return send(f"x{step}", value, lambda x, core, z, y: (x + step, 0, z, y) if core == 0 else None)

    def to_own(step, value):
        return send(f"d_own{step}", value, send_grads(step, True))

    def to_oth(step, value):
        return send(f"d_oth{step}", value, send_grads(step, False))

    low, high = to_x(1, totals[2][0]), to_x(3, totals[2][1])
    beside = [
        to_x(1, join("join_low", where, totals[1][0], low)),
        to_x(3, join("join_high", where, totals[3][0], high, SUB)),
    ]
    grads = [None] * 4
    grads[2] = (to_own(2, messages[4]), to_oth(2, messages[5]))
    totals[0] = input_grads(0, after(where, *grads[2]), cots, weights)
    grads[0] = (messages[0], to_oth(0, messages[1]))
    done = accumulate(2, where, acc_up, acc_down4, *grads[2], *masks, ())
    near_own = [to_own(step, after(messages[step * 2], *grads[2])) for step in (1, 3)]
    for step, own in zip((1, 3), near_own):
        grads[-step % 4] = (own, to_oth(step, after(messages[step * 2 + 1], *grads[2])))
    sums = [after(totals[0][0], *near_own, *done), *beside]
    part = sum(s.astype(F32) for s in sums).astype(BF16)
    pieces = [part[:, :KB]]
    for step in (1, 2, 3):
        pieces.append(
            send(
                f"y{step}",
                part[:, step * KB : (step + 1) * KB],
                lambda x, core, z, y: (x, 0, z, y + step) if core == 0 else None,
            )
        )
    both = sum(p.astype(F32) for p in pieces).astype(BF16)
    other = send("hand_over", both[SUB:], lambda x, core, z, y: (x, 1, z, y) if core == 0 else None)
    in_grad = jnp.where(first, both[:SUB], other)

    for step in (0, 3, 1):
        done = accumulate(step, where, acc_up, acc_down4, *grads[step], *masks, done)
    return (in_grad, done[0], done[1].reshape(acc_down.shape))


def solution(mesh):
    placed = (
        P("row", "col"),
        P("row", "col"),
        P("col", "row"),
        P("row", "col"),
        P("col", "row"),
        P("row", "col"),
        P("col", "row"),
        P("row", "col"),
    )
    return jax.shard_map(
        local,
        mesh=mesh,
        in_specs=placed,
        out_specs=(P("row", "col"), P("col", "row"), P("row", "col")),
        check_vma=False,
    )
```

```python
import math

import jax
import jax.numpy as jnp
from jax import lax
from jax.experimental import pallas as pl
from jax.experimental.pallas import tpu as pltpu
from jax.sharding import PartitionSpec as P

AXES = ("row", "col")
NT = (((1,), (1,)), ((), ()))
TN = (((0,), (0,)), ((), ()))
NN = (((1,), (0,)), ((), ()))
BF16 = jnp.bfloat16
F32 = jnp.float32
SCOPED = 20 * 1024 * 1024
KB = 384
SUB = 192
SEQ = 1536
ORDER = (2, 1, 3, 0)
PLAN = (("w", 0), ("w", 3), ("w", 1), ("i", 2), ("w", 2), ("i", 1), ("i", 3))


def ident(x, core, z, y):
    return ((x % 4 * 2 + core) * 4 + z % 4) * 4 + y % 4


def table(target):
    pairs = []
    for x in range(4):
        for core in range(2):
            for z in range(4):
                for y in range(4):
                    there = target(x, core, z, y)
                    if there is not None:
                        pairs.append((ident(x, core, z, y), ident(*there)))
    return pairs


def merge_to(step, role, x, core, z, y):
    return (x, role, z, y + step) if role == 0 else (x, role, z + step, y)


def reduce_to(step, role, x, core, z, y):
    return (x, role, z + step, y) if role == 0 else (x, role, z, y + step)


def send(name, value, target):
    with jax.named_scope(name):
        return lax.ppermute(value, AXES, table(target))


def send_weights(step, own):
    return lambda x, core, z, y: merge_to(step, core if own else 1 - core, x, core, z, y)


def send_reduce(step, own):
    def target(x, core, z, y):
        tx, _, tz, ty = reduce_to(step, core, x, core, z, y)
        return (tx, core if own else 1 - core, tz, ty)

    return target


def send_gather(step, own):
    return lambda x, core, z, y: reduce_to(step, core if own else 1 - core, x, core, z, y)


def send_grads(step, own):
    def target(x, core, z, y):
        tx, _, tz, ty = merge_to(step, core, x, core, z, y)
        return (tx, core if own else 1 - core, tz, ty)

    return target


SCALE = 5


def cost(flops, moved):
    return pl.CostEstimate(flops=flops // SCALE, bytes_accessed=moved // SCALE, transcendentals=0)


def call(name, body, grid, in_specs, out_specs, out_shape, flops, moved, aliases={}, scratch=()):
    return pl.pallas_call(
        body,
        name=name,
        grid_spec=pltpu.PrefetchScalarGridSpec(
            num_scalar_prefetch=1,
            grid=grid,
            in_specs=in_specs,
            out_specs=out_specs,
            scratch_shapes=list(scratch),
        ),
        out_shape=out_shape,
        input_output_aliases=aliases,
        compiler_params=pltpu.CompilerParams(vmem_limit_bytes=SCOPED),
        cost_estimate=cost(flops, moved),
    )


def after(value, *earlier):
    return lax.optimization_barrier((value, *earlier))[0]


def whole(shape):
    return pl.BlockSpec(shape, lambda i, s: (0,) * len(shape))


def one_hot(rows, cols, hit):
    r = lax.broadcasted_iota(jnp.int32, (rows, cols), 0)
    q = lax.broadcasted_iota(jnp.int32, (rows, cols), 1)
    return jnp.where(hit(r, q), 1.0, 0.0).astype(F32)


def mm(left, right, dims):
    return lax.dot_general(left, right, dims, preferred_element_type=F32)


def mod4(value):
    return lax.rem(value + 8, 4)


def spread_masks(where, mask_up, mask_down):
    def body(s, mu_ref, md_ref, up_out, down_out):
        y, z = s[0], s[1]
        wide_up = mm(mu_ref[...].astype(F32), one_hot(6, KB, lambda r, q: q // 64 == r), TN)
        wide_down = mm(md_ref[...].astype(F32), one_hot(6, KB, lambda r, q: q // 64 == r), NN)
        for step in range(4):
            pick = one_hot(
                12, 48, lambda r, q: q == (mod4(y + step) * 4 + mod4(z + r // 3)) * 3 + lax.rem(r, 3)
            )
            up_out[step] = mm(pick, wide_up, NN)
            pick = one_hot(
                12, 48, lambda r, q: q == (mod4(y + r // 3) * 4 + mod4(z + step)) * 3 + lax.rem(r, 3)
            )
            down_out[step] = mm(pick, wide_down, NN)

    shape = jax.ShapeDtypeStruct((4, 12, KB), F32)
    return resident("spread_masks", body, [shape] * 2, 10**6, 100_000)(where, mask_up, mask_down)


def prepare(where, w_up, w_down4, mask_up, mask_down):
    def body(s, up_hbm, down_hbm, mu_ref, md_ref, *refs):
        owns, oths, (up, down, turned, sem) = refs[:4], refs[4:8], refs[8:]
        y, z, core = s[0], s[1], s[2]
        copies = {}
        for step in ORDER:
            at = pl.multiple_of(mod4(y + step) * 4 * SUB, 4 * SUB)
            copies[step] = (
                pltpu.make_async_copy(up_hbm.at[:, pl.ds(at, 4 * SUB)], up.at[step], sem.at[step, 0]),
                pltpu.make_async_copy(down_hbm.at[:, mod4(z + step)], down.at[step], sem.at[step, 1]),
            )
            for copy in copies[step]:
                copy.start()

        for step in ORDER:
            mu, md = mu_ref[step].astype(BF16), md_ref[step].astype(BF16)
            for copy in copies[step]:
                copy.wait()
            turned[...] = up[step].T

            def put(up_out, down_out):
                for f in range(4):
                    at = pl.multiple_of(mod4(z + f) * SUB, SUB)
                    part = turned[pl.ds(at, SUB), :].reshape(3, 64, KB) * mu[f * 3 : f * 3 + 3][:, None, :]
                    up_out[f * SUB : (f + 1) * SUB, :] = part.reshape(SUB, KB)
                    part = down[step, mod4(y + f)].reshape(3, 64, KB) * md[f * 3 : f * 3 + 3][:, None, :]
                    down_out[f * SUB : (f + 1) * SUB, :] = part.reshape(SUB, KB)

            @pl.when(core == 0)
            def _():
                put(owns[step], oths[step])

            @pl.when(core != 0)
            def _():
                put(oths[step], owns[step])

    own_shape = jax.ShapeDtypeStruct((4 * SUB + KB, KB), BF16)
    oth_shape = jax.ShapeDtypeStruct((4 * SUB, KB), BF16)
    out = pl.pallas_call(
        body,
        name="prepare",
        in_specs=[pl.BlockSpec(memory_space=pltpu.SMEM)]
        + [pl.BlockSpec(memory_space=pltpu.HBM)] * 2
        + [pl.BlockSpec(memory_space=pltpu.VMEM)] * 2,
        out_specs=[pl.BlockSpec(memory_space=pltpu.VMEM)] * 8,
        out_shape=[own_shape] * 4 + [oth_shape] * 4,
        scratch_shapes=[
            pltpu.VMEM((4, KB, 4 * SUB), BF16),
            pltpu.VMEM((4, 4, SUB, KB), BF16),
            pltpu.VMEM((4 * SUB, KB), BF16),
            pltpu.SemaphoreType.DMA((4, 2)),
        ],
        compiler_params=pltpu.CompilerParams(vmem_limit_bytes=SCOPED),
        cost_estimate=cost(10**7, 9_600_000),
    )(where, w_up, w_down4, mask_up, mask_down)
    return list(out[:4]), list(out[4:])


def resident(name, body, out_shape, flops, moved, aliases={}):
    def make(where, *args):
        return pl.pallas_call(
            body,
            name=name,
            in_specs=[pl.BlockSpec(memory_space=pltpu.SMEM)] + [pl.BlockSpec(memory_space=pltpu.VMEM)] * len(args),
            out_specs=[pl.BlockSpec(memory_space=pltpu.VMEM)] * len(out_shape),
            out_shape=out_shape,
            input_output_aliases=aliases,
            compiler_params=pltpu.CompilerParams(vmem_limit_bytes=SCOPED),
            cost_estimate=cost(flops, moved),
        )(where, *args)

    return make


MATMUL = 2 * 384 * 1536 * 1536


def act_block(acts, weights, d, e):
    return weights[e * 2][4 * SUB :, :] if d == 2 else acts[d if d < 2 else 2][e]


def add_rows(where, buffers, rows):
    def body(s, *refs):
        for out in refs[5:]:
            out[4 * SUB :, :] = refs[4][...]

    shape = jax.ShapeDtypeStruct(buffers[0].shape, BF16)
    return resident("add_rows", body, [shape] * 4, 10**6, 1_000_000, {i + 1: i for i in range(4)})(where, *buffers, rows)


def flat(weights):
    return [weights[e][h] for e in range(4) for h in range(2)]


def forward(step, where, weights, acts):
    def body(s, *refs):
        w, a, o = refs[:8], refs[8:11], refs[11:]
        rows = slice(step * SUB, (step + 1) * SUB)
        left = jnp.concatenate(
            [jnp.concatenate([w[e * 2 + h][rows, :] for e in range(4)], axis=1) for h in range(2)], axis=0
        )
        for d in (0, 2):
            right = jnp.concatenate(
                [jnp.concatenate([act_block(a, w, dd, e) for e in range(4)], axis=1) for dd in (d, d + 1)], axis=0
            )
            total = mm(left, right, NT).astype(BF16)
            o[0][:, d * KB : (d + 2) * KB] = total[:SUB]
            o[1][:, d * KB : (d + 2) * KB] = total[SUB:]

    shape = jax.ShapeDtypeStruct((SUB, SEQ), BF16)
    return resident(f"partial{step}", body, [shape] * 2, MATMUL, 7_100_000)(where, *flat(weights), *acts)


def join(name, where, ours, theirs, at=0):
    def body(s, a, b, out):
        rows = slice(at, at + b.shape[0])
        out[rows, :] = (a[rows, :].astype(F32) + b[...].astype(F32)).astype(BF16)

    shape = jax.ShapeDtypeStruct(ours.shape, BF16)
    return resident(name, body, [shape], 10**6, 2_000_000, {1: 0})(where, ours, theirs)[0]


def gelu_parts(value):
    cdf = 0.5 * (1.0 + lax.erf(value / math.sqrt(2.0)))
    pdf = jnp.exp(-0.5 * value * value) / math.sqrt(2.0 * math.pi)
    return (value * cdf, cdf + value * pdf)


def activate(where, own, oth):
    def body(s, *refs):
        ins, (own_out, oth_out) = refs[:6], refs[6:]

        def put(rows, first, second, grad_out, hid_out):
            pre = sum(r[rows, :].astype(F32) for r in first)
            back = sum(r[rows, :].astype(F32) for r in second)
            act, slope = gelu_parts(pre)
            hid_out[rows, :] = act.astype(BF16)
            grad_out[rows, :] = (back * slope).astype(BF16)

        @pl.loop(0, SUB // 16)
        def _(i):
            rows = pl.ds(pl.multiple_of(i * 16, 16), 16)

            @pl.when(s[2] == 0)
            def _():
                put(rows, ins[:3], ins[3:], own_out, oth_out)

            @pl.when(s[2] != 0)
            def _():
                put(rows, ins[3:], ins[:3], oth_out, own_out)

    shape = jax.ShapeDtypeStruct((SUB, SEQ), BF16)
    return resident("activate", body, [shape] * 2, 10**7, 6_000_000)(where, *own, *oth)


def weight_grads(step, where, cots, weights, acts, before):
    def body(s, *refs):
        c, w, a, o = refs[:2], refs[2:10], refs[10:13], refs[-8:]
        left = jnp.concatenate([c[0][...], c[1][...]], axis=0)
        for e in (0, 2):
            right = jnp.concatenate(
                [jnp.concatenate([act_block(a, w, d, ee) for ee in (e, e + 1)], axis=1) for d in range(4)], axis=0
            )
            total = mm(left, right, NN).astype(BF16)
            for k in range(2):
                for h in range(2):
                    o[(e + k) * 2 + h][step] = total[h * SUB : (h + 1) * SUB, k * KB : (k + 1) * KB]

    shape = jax.ShapeDtypeStruct((4, SUB, KB), BF16)
    return resident(
        f"weight_grads{step}", body, [shape] * 8, MATMUL, 7_100_000, {14 + i: i for i in range(8)} if before else {}
    )(where, *cots, *flat(weights), *acts, *before)


def input_grads(step, where, cots, weights):
    def body(s, *refs):
        c, w, o = refs[:8], refs[8:16], refs[16:]

        @pl.when(s[2] == 0)
        def _():
            left = jnp.concatenate(
                [c[f * 2 + h][:, step * KB : (step + 1) * KB] for h in range(2) for f in range(4)], axis=0
            )
            for e in (0, 2):
                right = jnp.concatenate(
                    [
                        jnp.concatenate([w[ee * 2 + h][: 4 * SUB, :] for h in range(2)], axis=0)
                        for ee in (e, e + 1)
                    ],
                    axis=1,
                )
                total = mm(left, right, TN).astype(BF16)
                for i in range(len(o)):
                    o[i][:, e * KB : (e + 2) * KB] = total[i * rows : (i + 1) * rows]

        @pl.when(s[2] != 0)
        def _():
            for out in o:
                out[...] = jnp.zeros_like(out)

    rows = SUB if step == 2 else 2 * SUB
    shape = jax.ShapeDtypeStruct((rows, SEQ), BF16)
    return resident(f"input_grads{step}", body, [shape] * (2 * SUB // rows), MATMUL, 7_100_000)(
        where, *[cots[f][h] for f in range(4) for h in range(2)], *flat(weights)
    )


def accumulate(step, where, acc_up, acc_down4, own, oth, mask_up, mask_down, before):
    def body(s, up_ref, down_ref, own_ref, oth_ref, mu_ref, md_ref, *rest):
        up_out, down_out, wide = rest[-3:]
        y, z, core = s[0], s[1], s[2]
        mu = mu_ref[0].astype(BF16)
        md = md_ref[0]

        first = core == 0
        for f in range(4):
            own_part, oth_part = own_ref[f], oth_ref[f]
            to = pl.multiple_of(mod4(z + f) * SUB, SUB)
            part = jnp.where(first, own_part, oth_part).reshape(3, 64, 128) * mu[f * 3 : f * 3 + 3][:, None, :]
            wide[pl.ds(to, SUB), :] = part.reshape(SUB, 128)
            part = jnp.where(first, oth_part, own_part).astype(F32).reshape(3, 64, 128)
            part = (part * md[f * 3 : f * 3 + 3][:, None, :]).reshape(SUB, 128)
            down_out[mod4(y + f), 0] = down_ref[mod4(y + f), 0] + part

        up_out[...] = up_ref[...] + wide[...].T.astype(F32)

    up_block = pl.BlockSpec((128, 4 * SUB), lambda i, s: (i, mod4(s[0] + step)))
    down_block = pl.BlockSpec((4, 1, SUB, 128), lambda i, s: (0, mod4(s[1] + step), 0, i))
    mask_block = pl.BlockSpec((1, 12, 128), lambda i, s: (step, 0, i))
    grad_block = pl.BlockSpec((4, SUB, 128), lambda i, s: (0, 0, i))
    kept = list(before)
    return call(
        f"accumulate{step}",
        body,
        (3,),
        [up_block, down_block, grad_block, grad_block, mask_block, mask_block]
        + [pl.BlockSpec(memory_space=pl.ANY)] * len(kept),
        [up_block, down_block],
        [jax.ShapeDtypeStruct(acc_up.shape, F32), jax.ShapeDtypeStruct(acc_down4.shape, F32)],
        10**7,
        6_000_000,
        aliases={7: 0, 8: 1} if kept else {},
        scratch=[pltpu.VMEM((4 * SUB, 128), BF16)],
    )(where, acc_up, acc_down4, own, oth, mask_up, mask_down, *kept)


def local(tokens, out_grad, w_up, w_down, mask_up, mask_down, acc_up, acc_down):
    row, col = lax.axis_index("row"), lax.axis_index("col")
    core, z, y = lax.rem(row, 2), lax.div(col, 4), lax.rem(col, 4)
    where = jnp.stack([y, z, core]).astype(jnp.int32)
    first = core == 0
    w_down4 = pltpu.with_memory_space_constraint(w_down.reshape(4, 4, SUB, KB), pltpu.HBM)
    w_up = pltpu.with_memory_space_constraint(w_up, pltpu.HBM)
    acc_down4 = acc_down.reshape(4, 4, SUB, KB)

    away = send("swap", jnp.where(first, out_grad, tokens), lambda x, core, z, y: (x, 1 - core, z, y))
    mine = jnp.where(first, tokens, out_grad)
    masks = spread_masks(where, mask_up, mask_down)
    owns, oths = prepare(where, w_up, w_down4, *masks)
    block = jnp.concatenate([jnp.where(first, mine, away), jnp.where(first, away, mine)], axis=0)
    near = [block, None, None, None]
    for step in (1, 3, 2):
        near[-step % 4] = send(f"near{step}", block, lambda x, core, z, y: merge_to(step, core, x, core, z, y))
    block_far = send("opposite", block, lambda x, core, z, y: (x + 2, core, z, y))
    *near, block_far = lax.optimization_barrier((*near, block_far))
    acts = [jnp.stack(near), None, None]
    for step in (1, 3):
        acts[(-step % 4 + 1) // 2] = send(f"tokens{step}", acts[0], lambda x, core, z, y: (x + step, core, z, y))

    weights = [[None, None] for _ in range(4)]

    def oth_to(step, value):
        weights[-step % 4][1] = send(f"w_oth{step}", value, send_weights(step, False))
        return weights[-step % 4][1]

    def own_to(step, value):
        weights[-step % 4][0] = send(f"w_own{step}", value, send_weights(step, True))
        return weights[-step % 4][0]

    owns = add_rows(where, owns, block_far)
    weights[0][0] = owns[0]
    for step in ORDER:
        oth_to(step, oths[step] if step == 2 else after(oths[step], block_far))
    for step in (1, 3, 2):
        own_to(step, owns[step])

    parts, turn = {}, where
    for step in ORDER[:3]:
        parts[step] = forward(step, turn, weights, acts)
        turn = after(where, parts[step][1])

    def to_sum(step, value, own):
        return send(f"r{step}_{int(own)}", value, send_reduce(step, own))

    half_own, half_oth = to_sum(1, parts[2][0], True), to_sum(3, parts[2][1], True)
    oth_parts = [to_sum(1, parts[1][1], False)]
    own_parts = [to_sum(3, parts[3][0], True)]
    joined_own = join("join_own", where, parts[1][0], half_own)
    joined_oth = join("join_oth", where, parts[3][1], half_oth)
    own_parts.append(to_sum(1, joined_own, True))
    oth_parts.append(to_sum(3, joined_oth, False))
    parts[0] = forward(0, after(turn, joined_own, joined_oth), weights, acts)
    own_parts.append(parts[0][0])
    oth_parts.append(to_sum(0, parts[0][1], False))

    own, oth = activate(where, own_parts, oth_parts)

    def to_all(step, value, is_own):
        return send(f"g{step}_{int(is_own)}", value, send_gather(step, is_own))

    left_own, right_oth = to_all(1, own, True), to_all(3, oth, False)
    cots = [
        (own, to_all(0, oth, False)),
        (to_all(3, own, True), right_oth),
        (to_all(1, left_own, True), to_all(3, right_oth, True)),
        (left_own, to_all(1, oth, False)),
    ]

    messages, totals, turn = (), {}, where
    for kind, step in PLAN:
        if kind == "w":
            messages = weight_grads(step, turn, cots[step], weights, acts, messages)
            turn = after(where, messages[0])
        else:
            totals[step] = input_grads(step, turn, cots, weights)
            turn = after(where, totals[step][0])

    def to_x(step, value):
        return send(f"x{step}", value, lambda x, core, z, y: (x + step, 0, z, y) if core == 0 else None)

    def to_own(step, value):
        return send(f"d_own{step}", value, send_grads(step, True))

    def to_oth(step, value):
        return send(f"d_oth{step}", value, send_grads(step, False))

    low, high = to_x(1, totals[2][0]), to_x(3, totals[2][1])
    beside = [
        to_x(1, join("join_low", where, totals[1][0], low)),
        to_x(3, join("join_high", where, totals[3][0], high, SUB)),
    ]
    grads = [None] * 4
    grads[2] = (to_own(2, messages[4]), to_oth(2, messages[5]))
    totals[0] = input_grads(0, after(where, *grads[2]), cots, weights)
    grads[0] = (messages[0], to_oth(0, messages[1]))
    done = accumulate(0, where, acc_up, acc_down4, *grads[0], *masks, ())
    done = accumulate(2, where, acc_up, acc_down4, *grads[2], *masks, done)
    near_own = [to_own(step, after(messages[step * 2], *grads[2])) for step in (1, 3)]
    for step, own in zip((1, 3), near_own):
        grads[-step % 4] = (own, to_oth(step, after(messages[step * 2 + 1], *grads[2])))
    sums = [after(totals[0][0], *near_own, *done), *beside]
    part = sum(s.astype(F32) for s in sums).astype(BF16)
    pieces = [part[:, :KB]]
    for step in (1, 2, 3):
        pieces.append(
            send(
                f"y{step}",
                part[:, step * KB : (step + 1) * KB],
                lambda x, core, z, y: (x, 0, z, y + step) if core == 0 else None,
            )
        )
    done = accumulate(3, where, acc_up, acc_down4, *grads[3], *masks, done)
    pieces[0] = after(pieces[0], done[0])
    both = sum(p.astype(F32) for p in pieces).astype(BF16)
    other = send("hand_over", both[SUB:], lambda x, core, z, y: (x, 1, z, y) if core == 0 else None)
    in_grad = jnp.where(first, both[:SUB], other)
    done = accumulate(1, where, acc_up, acc_down4, *grads[1], *masks, done)
    return (in_grad, done[0], done[1].reshape(acc_down.shape))


def solution(mesh):
    placed = (
        P("row", "col"),
        P("row", "col"),
        P("col", "row"),
        P("row", "col"),
        P("col", "row"),
        P("row", "col"),
        P("col", "row"),
        P("row", "col"),
    )
    return jax.shard_map(
        local,
        mesh=mesh,
        in_specs=placed,
        out_specs=(P("row", "col"), P("col", "row"), P("row", "col")),
        check_vma=False,
    )
```

```python
import math

import jax
import jax.numpy as jnp
from jax import lax
from jax.experimental import pallas as pl
from jax.experimental.pallas import tpu as pltpu
from jax.sharding import PartitionSpec as P

AXES = ("row", "col")
NT = (((1,), (1,)), ((), ()))
TN = (((0,), (0,)), ((), ()))
NN = (((1,), (0,)), ((), ()))
BF16 = jnp.bfloat16
F32 = jnp.float32
SCOPED = 20 * 1024 * 1024
KB = 384
SUB = 192
SEQ = 1536
ORDER = (2, 1, 3, 0)
PLAN = (("w", 0), ("w", 3), ("w", 1), ("i", (2,)), ("w", 2), ("i", (1, 3)))


def ident(x, core, z, y):
    return ((x % 4 * 2 + core) * 4 + z % 4) * 4 + y % 4


def table(target):
    pairs = []
    for x in range(4):
        for core in range(2):
            for z in range(4):
                for y in range(4):
                    there = target(x, core, z, y)
                    if there is not None:
                        pairs.append((ident(x, core, z, y), ident(*there)))
    return pairs


def merge_to(step, role, x, core, z, y):
    return (x, role, z, y + step) if role == 0 else (x, role, z + step, y)


def reduce_to(step, role, x, core, z, y):
    return (x, role, z + step, y) if role == 0 else (x, role, z, y + step)


def send(name, value, target):
    with jax.named_scope(name):
        return lax.ppermute(value, AXES, table(target))


def send_weights(step, own):
    return lambda x, core, z, y: merge_to(step, core if own else 1 - core, x, core, z, y)


def send_reduce(step, own):
    def target(x, core, z, y):
        tx, _, tz, ty = reduce_to(step, core, x, core, z, y)
        return (tx, core if own else 1 - core, tz, ty)

    return target


def send_gather(step, own):
    return lambda x, core, z, y: reduce_to(step, core if own else 1 - core, x, core, z, y)


def send_grads(step, own):
    def target(x, core, z, y):
        tx, _, tz, ty = merge_to(step, core, x, core, z, y)
        return (tx, core if own else 1 - core, tz, ty)

    return target


SCALE = 5


def cost(flops, moved):
    return pl.CostEstimate(flops=flops // SCALE, bytes_accessed=moved // SCALE, transcendentals=0)


def call(name, body, grid, in_specs, out_specs, out_shape, flops, moved, aliases={}, scratch=()):
    return pl.pallas_call(
        body,
        name=name,
        grid_spec=pltpu.PrefetchScalarGridSpec(
            num_scalar_prefetch=1,
            grid=grid,
            in_specs=in_specs,
            out_specs=out_specs,
            scratch_shapes=list(scratch),
        ),
        out_shape=out_shape,
        input_output_aliases=aliases,
        compiler_params=pltpu.CompilerParams(vmem_limit_bytes=SCOPED),
        cost_estimate=cost(flops, moved),
    )


def after(value, *earlier):
    return lax.optimization_barrier((value, *earlier))[0]


def whole(shape):
    return pl.BlockSpec(shape, lambda i, s: (0,) * len(shape))


def one_hot(rows, cols, hit):
    r = lax.broadcasted_iota(jnp.int32, (rows, cols), 0)
    q = lax.broadcasted_iota(jnp.int32, (rows, cols), 1)
    return jnp.where(hit(r, q), 1.0, 0.0).astype(F32)


def mm(left, right, dims):
    return lax.dot_general(left, right, dims, preferred_element_type=F32)


def mod4(value):
    return lax.rem(value + 8, 4)


def spread_masks(where, mask_up, mask_down):
    def body(s, mu_ref, md_ref, up_out, down_out):
        y, z = s[0], s[1]
        wide_up = mm(mu_ref[...].astype(F32), one_hot(6, KB, lambda r, q: q // 64 == r), TN)
        wide_down = mm(md_ref[...].astype(F32), one_hot(6, KB, lambda r, q: q // 64 == r), NN)
        for step in range(4):
            pick = one_hot(
                12, 48, lambda r, q: q == (mod4(y + step) * 4 + mod4(z + r // 3)) * 3 + lax.rem(r, 3)
            )
            up_out[step] = mm(pick, wide_up, NN)
            pick = one_hot(
                12, 48, lambda r, q: q == (mod4(y + r // 3) * 4 + mod4(z + step)) * 3 + lax.rem(r, 3)
            )
            down_out[step] = mm(pick, wide_down, NN)

    shape = jax.ShapeDtypeStruct((4, 12, KB), F32)
    return resident("spread_masks", body, [shape] * 2, 10**6, 100_000)(where, mask_up, mask_down)


def prepare(where, w_up, w_down4, mask_up, mask_down):
    def body(s, up_hbm, down_hbm, mu_ref, md_ref, *refs):
        owns, oths, (up, down, turned, sem) = refs[:4], refs[4:8], refs[8:]
        y, z, core = s[0], s[1], s[2]
        copies = {}
        for step in ORDER:
            at = pl.multiple_of(mod4(y + step) * 4 * SUB, 4 * SUB)
            copies[step] = (
                pltpu.make_async_copy(up_hbm.at[:, pl.ds(at, 4 * SUB)], up.at[step], sem.at[step, 0]),
                pltpu.make_async_copy(down_hbm.at[:, mod4(z + step)], down.at[step], sem.at[step, 1]),
            )
            for copy in copies[step]:
                copy.start()

        for step in ORDER:
            mu, md = mu_ref[step].astype(BF16), md_ref[step].astype(BF16)
            for copy in copies[step]:
                copy.wait()
            turned[...] = up[step].T

            def put(up_out, down_out):
                for f in range(4):
                    at = pl.multiple_of(mod4(z + f) * SUB, SUB)
                    part = turned[pl.ds(at, SUB), :].reshape(3, 64, KB) * mu[f * 3 : f * 3 + 3][:, None, :]
                    up_out[f * SUB : (f + 1) * SUB, :] = part.reshape(SUB, KB)
                    part = down[step, mod4(y + f)].reshape(3, 64, KB) * md[f * 3 : f * 3 + 3][:, None, :]
                    down_out[f * SUB : (f + 1) * SUB, :] = part.reshape(SUB, KB)

            @pl.when(core == 0)
            def _():
                put(owns[step], oths[step])

            @pl.when(core != 0)
            def _():
                put(oths[step], owns[step])

    own_shape = jax.ShapeDtypeStruct((4 * SUB + KB, KB), BF16)
    oth_shape = jax.ShapeDtypeStruct((4 * SUB, KB), BF16)
    out = pl.pallas_call(
        body,
        name="prepare",
        in_specs=[pl.BlockSpec(memory_space=pltpu.SMEM)]
        + [pl.BlockSpec(memory_space=pltpu.HBM)] * 2
        + [pl.BlockSpec(memory_space=pltpu.VMEM)] * 2,
        out_specs=[pl.BlockSpec(memory_space=pltpu.VMEM)] * 8,
        out_shape=[own_shape] * 4 + [oth_shape] * 4,
        scratch_shapes=[
            pltpu.VMEM((4, KB, 4 * SUB), BF16),
            pltpu.VMEM((4, 4, SUB, KB), BF16),
            pltpu.VMEM((4 * SUB, KB), BF16),
            pltpu.SemaphoreType.DMA((4, 2)),
        ],
        compiler_params=pltpu.CompilerParams(vmem_limit_bytes=SCOPED),
        cost_estimate=cost(10**7, 9_600_000),
    )(where, w_up, w_down4, mask_up, mask_down)
    return list(out[:4]), list(out[4:])


def resident(name, body, out_shape, flops, moved, aliases={}):
    def make(where, *args):
        return pl.pallas_call(
            body,
            name=name,
            in_specs=[pl.BlockSpec(memory_space=pltpu.SMEM)] + [pl.BlockSpec(memory_space=pltpu.VMEM)] * len(args),
            out_specs=[pl.BlockSpec(memory_space=pltpu.VMEM)] * len(out_shape),
            out_shape=out_shape,
            input_output_aliases=aliases,
            compiler_params=pltpu.CompilerParams(vmem_limit_bytes=SCOPED),
            cost_estimate=cost(flops, moved),
        )(where, *args)

    return make


MATMUL = 2 * 384 * 1536 * 1536


def act_block(acts, weights, d, e):
    return weights[e * 2][4 * SUB :, :] if d == 2 else acts[d if d < 2 else 2][e]


def add_rows(where, buffers, rows):
    def body(s, *refs):
        for out in refs[5:]:
            out[4 * SUB :, :] = refs[4][...]

    shape = jax.ShapeDtypeStruct(buffers[0].shape, BF16)
    return resident("add_rows", body, [shape] * 4, 10**6, 1_000_000, {i + 1: i for i in range(4)})(where, *buffers, rows)


def flat(weights):
    return [weights[e][h] for e in range(4) for h in range(2)]


def forward(step, where, weights, acts):
    def body(s, *refs):
        w, a, o = refs[:8], refs[8:11], refs[11:]
        rows = slice(step * SUB, (step + 1) * SUB)
        left = jnp.concatenate(
            [jnp.concatenate([w[e * 2 + h][rows, :] for e in range(4)], axis=1) for h in range(2)], axis=0
        )
        for d in (0, 2):
            right = jnp.concatenate(
                [jnp.concatenate([act_block(a, w, dd, e) for e in range(4)], axis=1) for dd in (d, d + 1)], axis=0
            )
            total = mm(left, right, NT).astype(BF16)
            o[0][:, d * KB : (d + 2) * KB] = total[:SUB]
            o[1][:, d * KB : (d + 2) * KB] = total[SUB:]

    shape = jax.ShapeDtypeStruct((SUB, SEQ), BF16)
    return resident(f"partial{step}", body, [shape] * 2, MATMUL, 7_100_000)(where, *flat(weights), *acts)


def join(name, where, first, first_part, second, second_part, at=0):
    def body(s, a, part_a, b, part_b, out_a, out_b):
        for ours, theirs, out, row in ((a, part_a, out_a, 0), (b, part_b, out_b, at)):
            rows = slice(row, row + theirs.shape[0])
            out[rows, :] = (ours[rows, :].astype(F32) + theirs[...].astype(F32)).astype(BF16)

    shape = jax.ShapeDtypeStruct(first.shape, BF16)
    return resident(name, body, [shape] * 2, 10**6, 4_000_000, {1: 0, 3: 1})(
        where, first, first_part, second, second_part
    )


def gelu_parts(value):
    cdf = 0.5 * (1.0 + lax.erf(value / math.sqrt(2.0)))
    pdf = jnp.exp(-0.5 * value * value) / math.sqrt(2.0 * math.pi)
    return (value * cdf, cdf + value * pdf)


def activate(where, own, oth):
    def body(s, *refs):
        ins, (own_out, oth_out) = refs[:6], refs[6:]

        def put(rows, first, second, grad_out, hid_out):
            pre = sum(r[rows, :].astype(F32) for r in first)
            back = sum(r[rows, :].astype(F32) for r in second)
            act, slope = gelu_parts(pre)
            hid_out[rows, :] = act.astype(BF16)
            grad_out[rows, :] = (back * slope).astype(BF16)

        @pl.loop(0, SUB // 16)
        def _(i):
            rows = pl.ds(pl.multiple_of(i * 16, 16), 16)

            @pl.when(s[2] == 0)
            def _():
                put(rows, ins[:3], ins[3:], own_out, oth_out)

            @pl.when(s[2] != 0)
            def _():
                put(rows, ins[3:], ins[:3], oth_out, own_out)

    shape = jax.ShapeDtypeStruct((SUB, SEQ), BF16)
    return resident("activate", body, [shape] * 2, 10**7, 6_000_000)(where, *own, *oth)


def weight_grads(step, where, cots, weights, acts, before):
    def body(s, *refs):
        c, w, a, o = refs[:2], refs[2:10], refs[10:13], refs[-8:]
        left = jnp.concatenate([c[0][...], c[1][...]], axis=0)
        for e in (0, 2):
            right = jnp.concatenate(
                [jnp.concatenate([act_block(a, w, d, ee) for ee in (e, e + 1)], axis=1) for d in range(4)], axis=0
            )
            total = mm(left, right, NN).astype(BF16)
            for k in range(2):
                for h in range(2):
                    o[(e + k) * 2 + h][step] = total[h * SUB : (h + 1) * SUB, k * KB : (k + 1) * KB]

    shape = jax.ShapeDtypeStruct((4, SUB, KB), BF16)
    return resident(
        f"weight_grads{step}", body, [shape] * 8, MATMUL, 7_100_000, {14 + i: i for i in range(8)} if before else {}
    )(where, *cots, *flat(weights), *acts, *before)


def input_grads(steps, where, cots, weights):
    def body(s, *refs):
        c, w, o = refs[:8], refs[8:16], refs[16:]

        @pl.when(s[2] == 0)
        def _():
            for k, step in enumerate(steps):
                outs = o if step == 2 else o[k : k + 1]
                left = jnp.concatenate(
                    [c[f * 2 + h][:, step * KB : (step + 1) * KB] for h in range(2) for f in range(4)], axis=0
                )
                for e in (0, 2):
                    right = jnp.concatenate(
                        [
                            jnp.concatenate([w[ee * 2 + h][: 4 * SUB, :] for h in range(2)], axis=0)
                            for ee in (e, e + 1)
                        ],
                        axis=1,
                    )
                    total = mm(left, right, TN).astype(BF16)
                    for i, out in enumerate(outs):
                        out[:, e * KB : (e + 2) * KB] = total[i * rows : (i + 1) * rows]

        @pl.when(s[2] != 0)
        def _():
            for out in o:
                out[...] = jnp.zeros_like(out)

    rows, count = (SUB, 2) if steps == (2,) else (2 * SUB, len(steps))
    shape = jax.ShapeDtypeStruct((rows, SEQ), BF16)
    name = "input_grads" + "".join(str(step) for step in steps)
    return resident(name, body, [shape] * count, MATMUL * len(steps), 7_100_000)(
        where, *[cots[f][h] for f in range(4) for h in range(2)], *flat(weights)
    )


def accumulate(step, where, acc_up, acc_down4, own, oth, mask_up, mask_down, before):
    def body(s, up_ref, down_ref, own_ref, oth_ref, mu_ref, md_ref, *rest):
        up_out, down_out, wide = rest[-3:]
        y, z, core = s[0], s[1], s[2]
        mu = mu_ref[0].astype(BF16)
        md = md_ref[0]

        first = core == 0
        for f in range(4):
            own_part, oth_part = own_ref[f], oth_ref[f]
            to = pl.multiple_of(mod4(z + f) * SUB, SUB)
            part = jnp.where(first, own_part, oth_part).reshape(3, 64, 128) * mu[f * 3 : f * 3 + 3][:, None, :]
            wide[pl.ds(to, SUB), :] = part.reshape(SUB, 128)
            part = jnp.where(first, oth_part, own_part).astype(F32).reshape(3, 64, 128)
            part = (part * md[f * 3 : f * 3 + 3][:, None, :]).reshape(SUB, 128)
            down_out[mod4(y + f), 0] = down_ref[mod4(y + f), 0] + part

        up_out[...] = up_ref[...] + wide[...].T.astype(F32)

    up_block = pl.BlockSpec((128, 4 * SUB), lambda i, s: (i, mod4(s[0] + step)))
    down_block = pl.BlockSpec((4, 1, SUB, 128), lambda i, s: (0, mod4(s[1] + step), 0, i))
    mask_block = pl.BlockSpec((1, 12, 128), lambda i, s: (step, 0, i))
    grad_block = pl.BlockSpec((4, SUB, 128), lambda i, s: (0, 0, i))
    kept = list(before)
    return call(
        f"accumulate{step}",
        body,
        (3,),
        [up_block, down_block, grad_block, grad_block, mask_block, mask_block]
        + [pl.BlockSpec(memory_space=pl.ANY)] * len(kept),
        [up_block, down_block],
        [jax.ShapeDtypeStruct(acc_up.shape, F32), jax.ShapeDtypeStruct(acc_down4.shape, F32)],
        10**7,
        6_000_000,
        aliases={7: 0, 8: 1} if kept else {},
        scratch=[pltpu.VMEM((4 * SUB, 128), BF16)],
    )(where, acc_up, acc_down4, own, oth, mask_up, mask_down, *kept)


def local(tokens, out_grad, w_up, w_down, mask_up, mask_down, acc_up, acc_down):
    row, col = lax.axis_index("row"), lax.axis_index("col")
    core, z, y = lax.rem(row, 2), lax.div(col, 4), lax.rem(col, 4)
    where = jnp.stack([y, z, core]).astype(jnp.int32)
    first = core == 0
    w_down4 = pltpu.with_memory_space_constraint(w_down.reshape(4, 4, SUB, KB), pltpu.HBM)
    w_up = pltpu.with_memory_space_constraint(w_up, pltpu.HBM)
    acc_down4 = acc_down.reshape(4, 4, SUB, KB)

    away = send("swap", jnp.where(first, out_grad, tokens), lambda x, core, z, y: (x, 1 - core, z, y))
    mine = jnp.where(first, tokens, out_grad)
    masks = spread_masks(where, mask_up, mask_down)
    owns, oths = prepare(where, w_up, w_down4, *masks)
    block = jnp.concatenate([jnp.where(first, mine, away), jnp.where(first, away, mine)], axis=0)
    near = [block, None, None, None]
    for step in (1, 3, 2):
        near[-step % 4] = send(f"near{step}", block, lambda x, core, z, y: merge_to(step, core, x, core, z, y))
    block_far = send("opposite", block, lambda x, core, z, y: (x + 2, core, z, y))
    *near, block_far = lax.optimization_barrier((*near, block_far))
    acts = [jnp.stack(near), None, None]
    for step in (1, 3):
        acts[(-step % 4 + 1) // 2] = send(f"tokens{step}", acts[0], lambda x, core, z, y: (x + step, core, z, y))

    weights = [[None, None] for _ in range(4)]

    def oth_to(step, value):
        weights[-step % 4][1] = send(f"w_oth{step}", value, send_weights(step, False))
        return weights[-step % 4][1]

    def own_to(step, value):
        weights[-step % 4][0] = send(f"w_own{step}", value, send_weights(step, True))
        return weights[-step % 4][0]

    owns = add_rows(where, owns, block_far)
    weights[0][0] = owns[0]
    for step in ORDER:
        oth_to(step, oths[step] if step == 2 else after(oths[step], block_far))
    for step in (1, 3, 2):
        own_to(step, owns[step])

    parts, turn = {}, where
    for step in ORDER[:3]:
        parts[step] = forward(step, turn, weights, acts)
        turn = after(where, parts[step][1])

    def to_sum(step, value, own):
        return send(f"r{step}_{int(own)}", value, send_reduce(step, own))

    half_own, half_oth = to_sum(1, parts[2][0], True), to_sum(3, parts[2][1], True)
    oth_parts = [to_sum(1, parts[1][1], False)]
    own_parts = [to_sum(3, parts[3][0], True)]
    joined_own, joined_oth = join("join_sums", where, parts[1][0], half_own, parts[3][1], half_oth)
    own_parts.append(to_sum(1, joined_own, True))
    oth_parts.append(to_sum(3, joined_oth, False))
    parts[0] = forward(0, after(turn, joined_own, joined_oth), weights, acts)
    own_parts.append(parts[0][0])
    oth_parts.append(to_sum(0, parts[0][1], False))

    own, oth = activate(where, own_parts, oth_parts)

    def to_all(step, value, is_own):
        return send(f"g{step}_{int(is_own)}", value, send_gather(step, is_own))

    left_own, right_oth = to_all(1, own, True), to_all(3, oth, False)
    cots = [
        (own, to_all(0, oth, False)),
        (to_all(3, own, True), right_oth),
        (to_all(1, left_own, True), to_all(3, right_oth, True)),
        (left_own, to_all(1, oth, False)),
    ]

    messages, totals, turn = (), {}, where
    for kind, step in PLAN:
        if kind == "w":
            messages = weight_grads(step, turn, cots[step], weights, acts, messages)
            turn = after(where, messages[0])
        else:
            totals[step] = input_grads(step, turn, cots, weights)
            turn = after(where, totals[step][0])

    ahead, behind = totals[(1, 3)]

    def to_x(step, value):
        return send(f"x{step}", value, lambda x, core, z, y: (x + step, 0, z, y) if core == 0 else None)

    def to_own(step, value):
        return send(f"d_own{step}", value, send_grads(step, True))

    def to_oth(step, value):
        return send(f"d_oth{step}", value, send_grads(step, False))

    low, high = to_x(1, totals[(2,)][0]), to_x(3, totals[(2,)][1])
    joined_low, joined_high = join("join_inputs", where, ahead, low, behind, high, SUB)
    beside = [to_x(1, joined_low), to_x(3, joined_high)]
    grads = [None] * 4
    grads[2] = (to_own(2, messages[4]), to_oth(2, messages[5]))
    (here,) = input_grads((0,), after(where, *grads[2]), cots, weights)
    grads[0] = (messages[0], to_oth(0, messages[1]))
    done = accumulate(0, where, acc_up, acc_down4, *grads[0], *masks, ())
    done = accumulate(2, where, acc_up, acc_down4, *grads[2], *masks, done)
    near_own = [to_own(step, after(messages[step * 2], *grads[2])) for step in (1, 3)]
    for step, own in zip((1, 3), near_own):
        grads[-step % 4] = (own, to_oth(step, after(messages[step * 2 + 1], *grads[2])))
    sums = [after(here, *near_own, *done), *beside]
    part = sum(s.astype(F32) for s in sums).astype(BF16)
    pieces = [part[:, :KB]]
    for step in (1, 2, 3):
        pieces.append(
            send(
                f"y{step}",
                part[:, step * KB : (step + 1) * KB],
                lambda x, core, z, y: (x, 0, z, y + step) if core == 0 else None,
            )
        )
    done = accumulate(3, where, acc_up, acc_down4, *grads[3], *masks, done)
    pieces[0] = after(pieces[0], done[0])
    both = sum(p.astype(F32) for p in pieces).astype(BF16)
    other = send("hand_over", both[SUB:], lambda x, core, z, y: (x, 1, z, y) if core == 0 else None)
    in_grad = jnp.where(first, both[:SUB], other)
    done = accumulate(1, where, acc_up, acc_down4, *grads[1], *masks, done)
    return (in_grad, done[0], done[1].reshape(acc_down.shape))


def solution(mesh):
    placed = (
        P("row", "col"),
        P("row", "col"),
        P("col", "row"),
        P("row", "col"),
        P("col", "row"),
        P("row", "col"),
        P("col", "row"),
        P("row", "col"),
    )
    return jax.shard_map(
        local,
        mesh=mesh,
        in_specs=placed,
        out_specs=(P("row", "col"), P("col", "row"), P("row", "col")),
        check_vma=False,
    )
```

```python
import math

import jax
import jax.numpy as jnp
from jax import lax
from jax.experimental import pallas as pl
from jax.experimental.pallas import tpu as pltpu
from jax.sharding import PartitionSpec as P

AXES = ("row", "col")
NT = (((1,), (1,)), ((), ()))
TN = (((0,), (0,)), ((), ()))
NN = (((1,), (0,)), ((), ()))
BF16 = jnp.bfloat16
F32 = jnp.float32
SCOPED = 20 * 1024 * 1024
KB = 384
SUB = 192
SEQ = 1536
ORDER = (2, 1, 3, 0)
PLAN = (("w", 0), ("w", 3), ("w", 1), ("i", (2,)), ("w", 2), ("i", (1, 3)))


def ident(x, core, z, y):
    return ((x % 4 * 2 + core) * 4 + z % 4) * 4 + y % 4


def table(target):
    pairs = []
    for x in range(4):
        for core in range(2):
            for z in range(4):
                for y in range(4):
                    there = target(x, core, z, y)
                    if there is not None:
                        pairs.append((ident(x, core, z, y), ident(*there)))
    return pairs


def merge_to(step, role, x, core, z, y):
    return (x, role, z, y + step) if role == 0 else (x, role, z + step, y)


def reduce_to(step, role, x, core, z, y):
    return (x, role, z + step, y) if role == 0 else (x, role, z, y + step)


def send(name, value, target):
    with jax.named_scope(name):
        return lax.ppermute(value, AXES, table(target))


def send_weights(step, own):
    return lambda x, core, z, y: merge_to(step, core if own else 1 - core, x, core, z, y)


def send_reduce(step, own):
    def target(x, core, z, y):
        tx, _, tz, ty = reduce_to(step, core, x, core, z, y)
        return (tx, core if own else 1 - core, tz, ty)

    return target


def send_gather(step, own):
    return lambda x, core, z, y: reduce_to(step, core if own else 1 - core, x, core, z, y)


def send_grads(step, own):
    def target(x, core, z, y):
        tx, _, tz, ty = merge_to(step, core, x, core, z, y)
        return (tx, core if own else 1 - core, tz, ty)

    return target


SCALE = 5


def cost(flops, moved):
    return pl.CostEstimate(flops=flops // SCALE, bytes_accessed=moved // SCALE, transcendentals=0)


def call(name, body, grid, in_specs, out_specs, out_shape, flops, moved, aliases={}, scratch=()):
    return pl.pallas_call(
        body,
        name=name,
        grid_spec=pltpu.PrefetchScalarGridSpec(
            num_scalar_prefetch=1,
            grid=grid,
            in_specs=in_specs,
            out_specs=out_specs,
            scratch_shapes=list(scratch),
        ),
        out_shape=out_shape,
        input_output_aliases=aliases,
        compiler_params=pltpu.CompilerParams(vmem_limit_bytes=SCOPED),
        cost_estimate=cost(flops, moved),
    )


def after(value, *earlier):
    return lax.optimization_barrier((value, *earlier))[0]


def whole(shape):
    return pl.BlockSpec(shape, lambda i, s: (0,) * len(shape))


def one_hot(rows, cols, hit):
    r = lax.broadcasted_iota(jnp.int32, (rows, cols), 0)
    q = lax.broadcasted_iota(jnp.int32, (rows, cols), 1)
    return jnp.where(hit(r, q), 1.0, 0.0).astype(F32)


def mm(left, right, dims):
    return lax.dot_general(left, right, dims, preferred_element_type=F32)


def mod4(value):
    return lax.rem(value + 8, 4)


def spread_masks(y, z, mu_ref, md_ref, up_out, down_out):
    wide_up = mm(mu_ref[...].astype(F32), one_hot(6, KB, lambda r, q: q // 64 == r), TN)
    wide_down = mm(md_ref[...].astype(F32), one_hot(6, KB, lambda r, q: q // 64 == r), NN)
    for step in range(4):
        pick = one_hot(12, 48, lambda r, q: q == (mod4(y + step) * 4 + mod4(z + r // 3)) * 3 + lax.rem(r, 3))
        up_out[step] = mm(pick, wide_up, NN)
        pick = one_hot(12, 48, lambda r, q: q == (mod4(y + r // 3) * 4 + mod4(z + step)) * 3 + lax.rem(r, 3))
        down_out[step] = mm(pick, wide_down, NN)


def prepare(where, w_up, w_down4, mask_up, mask_down):
    def body(s, up_hbm, down_hbm, mu_ref, md_ref, *refs):
        owns, oths, (up_masks, down_masks, up, down, turned, sem) = refs[:4], refs[4:8], refs[8:]
        y, z, core = s[0], s[1], s[2]
        copies = {}
        for step in ORDER:
            at = pl.multiple_of(mod4(y + step) * 4 * SUB, 4 * SUB)
            copies[step] = (
                pltpu.make_async_copy(up_hbm.at[:, pl.ds(at, 4 * SUB)], up.at[step], sem.at[step, 0]),
                pltpu.make_async_copy(down_hbm.at[:, mod4(z + step)], down.at[step], sem.at[step, 1]),
            )
            for copy in copies[step]:
                copy.start()

        spread_masks(y, z, mu_ref, md_ref, up_masks, down_masks)
        for step in ORDER:
            mu, md = up_masks[step].astype(BF16), down_masks[step].astype(BF16)
            for copy in copies[step]:
                copy.wait()
            turned[...] = up[step].T

            def put(up_out, down_out):
                for f in range(4):
                    at = pl.multiple_of(mod4(z + f) * SUB, SUB)
                    part = turned[pl.ds(at, SUB), :].reshape(3, 64, KB) * mu[f * 3 : f * 3 + 3][:, None, :]
                    up_out[f * SUB : (f + 1) * SUB, :] = part.reshape(SUB, KB)
                    part = down[step, mod4(y + f)].reshape(3, 64, KB) * md[f * 3 : f * 3 + 3][:, None, :]
                    down_out[f * SUB : (f + 1) * SUB, :] = part.reshape(SUB, KB)

            @pl.when(core == 0)
            def _():
                put(owns[step], oths[step])

            @pl.when(core != 0)
            def _():
                put(oths[step], owns[step])

    own_shape = jax.ShapeDtypeStruct((4 * SUB + KB, KB), BF16)
    oth_shape = jax.ShapeDtypeStruct((4 * SUB, KB), BF16)
    out = pl.pallas_call(
        body,
        name="prepare",
        in_specs=[pl.BlockSpec(memory_space=pltpu.SMEM)]
        + [pl.BlockSpec(memory_space=pltpu.HBM)] * 2
        + [pl.BlockSpec(memory_space=pltpu.VMEM)] * 2,
        out_specs=[pl.BlockSpec(memory_space=pltpu.VMEM)] * 10,
        out_shape=[own_shape] * 4 + [oth_shape] * 4 + [jax.ShapeDtypeStruct((4, 12, KB), F32)] * 2,
        scratch_shapes=[
            pltpu.VMEM((4, KB, 4 * SUB), BF16),
            pltpu.VMEM((4, 4, SUB, KB), BF16),
            pltpu.VMEM((4 * SUB, KB), BF16),
            pltpu.SemaphoreType.DMA((4, 2)),
        ],
        compiler_params=pltpu.CompilerParams(vmem_limit_bytes=SCOPED),
        cost_estimate=cost(10**7, 9_600_000),
    )(where, w_up, w_down4, mask_up, mask_down)
    return list(out[:4]), list(out[4:8]), out[8:]


def resident(name, body, out_shape, flops, moved, aliases={}):
    def make(where, *args):
        return pl.pallas_call(
            body,
            name=name,
            in_specs=[pl.BlockSpec(memory_space=pltpu.SMEM)] + [pl.BlockSpec(memory_space=pltpu.VMEM)] * len(args),
            out_specs=[pl.BlockSpec(memory_space=pltpu.VMEM)] * len(out_shape),
            out_shape=out_shape,
            input_output_aliases=aliases,
            compiler_params=pltpu.CompilerParams(vmem_limit_bytes=SCOPED),
            cost_estimate=cost(flops, moved),
        )(where, *args)

    return make


MATMUL = 2 * 384 * 1536 * 1536


def act_block(acts, weights, d, e):
    return weights[e * 2][4 * SUB :, :] if d == 2 else acts[d if d < 2 else 2][e]


def add_rows(where, buffers, rows):
    def body(s, *refs):
        for out in refs[5:]:
            out[4 * SUB :, :] = refs[4][...]

    shape = jax.ShapeDtypeStruct(buffers[0].shape, BF16)
    return resident("add_rows", body, [shape] * 4, 10**6, 1_000_000, {i + 1: i for i in range(4)})(where, *buffers, rows)


def flat(weights):
    return [weights[e][h] for e in range(4) for h in range(2)]


def forward(step, where, weights, acts):
    def body(s, *refs):
        w, a, o = refs[:8], refs[8:11], refs[11:]
        rows = slice(step * SUB, (step + 1) * SUB)
        left = jnp.concatenate(
            [jnp.concatenate([w[e * 2 + h][rows, :] for e in range(4)], axis=1) for h in range(2)], axis=0
        )
        for d in (0, 2):
            right = jnp.concatenate(
                [jnp.concatenate([act_block(a, w, dd, e) for e in range(4)], axis=1) for dd in (d, d + 1)], axis=0
            )
            total = mm(left, right, NT).astype(BF16)
            o[0][:, d * KB : (d + 2) * KB] = total[:SUB]
            o[1][:, d * KB : (d + 2) * KB] = total[SUB:]

    shape = jax.ShapeDtypeStruct((SUB, SEQ), BF16)
    return resident(f"partial{step}", body, [shape] * 2, MATMUL, 7_100_000)(where, *flat(weights), *acts)


def join(name, where, first, first_part, second, second_part, at=0):
    def body(s, a, part_a, b, part_b, out_a, out_b):
        for ours, theirs, out, row in ((a, part_a, out_a, 0), (b, part_b, out_b, at)):
            rows = slice(row, row + theirs.shape[0])
            out[rows, :] = (ours[rows, :].astype(F32) + theirs[...].astype(F32)).astype(BF16)

    shape = jax.ShapeDtypeStruct(first.shape, BF16)
    return resident(name, body, [shape] * 2, 10**6, 4_000_000, {1: 0, 3: 1})(
        where, first, first_part, second, second_part
    )


def gelu_parts(value):
    cdf = 0.5 * (1.0 + lax.erf(value / math.sqrt(2.0)))
    pdf = jnp.exp(-0.5 * value * value) / math.sqrt(2.0 * math.pi)
    return (value * cdf, cdf + value * pdf)


def activate(where, own, oth):
    def body(s, *refs):
        ins, (own_out, oth_out) = refs[:6], refs[6:]

        def put(rows, first, second, grad_out, hid_out):
            pre = sum(r[rows, :].astype(F32) for r in first)
            back = sum(r[rows, :].astype(F32) for r in second)
            act, slope = gelu_parts(pre)
            hid_out[rows, :] = act.astype(BF16)
            grad_out[rows, :] = (back * slope).astype(BF16)

        @pl.loop(0, SUB // 16)
        def _(i):
            rows = pl.ds(pl.multiple_of(i * 16, 16), 16)

            @pl.when(s[2] == 0)
            def _():
                put(rows, ins[:3], ins[3:], own_out, oth_out)

            @pl.when(s[2] != 0)
            def _():
                put(rows, ins[3:], ins[:3], oth_out, own_out)

    shape = jax.ShapeDtypeStruct((SUB, SEQ), BF16)
    return resident("activate", body, [shape] * 2, 10**7, 6_000_000)(where, *own, *oth)


def weight_grads(step, where, cots, weights, acts, before):
    def body(s, *refs):
        c, w, a, o = refs[:2], refs[2:10], refs[10:13], refs[-8:]
        left = jnp.concatenate([c[0][...], c[1][...]], axis=0)
        for e in (0, 2):
            right = jnp.concatenate(
                [jnp.concatenate([act_block(a, w, d, ee) for ee in (e, e + 1)], axis=1) for d in range(4)], axis=0
            )
            total = mm(left, right, NN).astype(BF16)
            for k in range(2):
                for h in range(2):
                    o[(e + k) * 2 + h][step] = total[h * SUB : (h + 1) * SUB, k * KB : (k + 1) * KB]

    shape = jax.ShapeDtypeStruct((4, SUB, KB), BF16)
    return resident(
        f"weight_grads{step}", body, [shape] * 8, MATMUL, 7_100_000, {14 + i: i for i in range(8)} if before else {}
    )(where, *cots, *flat(weights), *acts, *before)


def input_grads(steps, where, cots, weights):
    def body(s, *refs):
        c, w, o = refs[:8], refs[8:16], refs[16:]

        @pl.when(s[2] == 0)
        def _():
            for k, step in enumerate(steps):
                outs = o if step == 2 else o[k : k + 1]
                left = jnp.concatenate(
                    [c[f * 2 + h][:, step * KB : (step + 1) * KB] for h in range(2) for f in range(4)], axis=0
                )
                for e in (0, 2):
                    right = jnp.concatenate(
                        [
                            jnp.concatenate([w[ee * 2 + h][: 4 * SUB, :] for h in range(2)], axis=0)
                            for ee in (e, e + 1)
                        ],
                        axis=1,
                    )
                    total = mm(left, right, TN).astype(BF16)
                    for i, out in enumerate(outs):
                        out[:, e * KB : (e + 2) * KB] = total[i * rows : (i + 1) * rows]

        @pl.when(s[2] != 0)
        def _():
            for out in o:
                out[...] = jnp.zeros_like(out)

    rows, count = (SUB, 2) if steps == (2,) else (2 * SUB, len(steps))
    shape = jax.ShapeDtypeStruct((rows, SEQ), BF16)
    name = "input_grads" + "".join(str(step) for step in steps)
    return resident(name, body, [shape] * count, MATMUL * len(steps), 7_100_000)(
        where, *[cots[f][h] for f in range(4) for h in range(2)], *flat(weights)
    )


def accumulate(step, where, acc_up, acc_down4, own, oth, mask_up, mask_down, before):
    def body(s, up_ref, down_ref, own_ref, oth_ref, mu_ref, md_ref, *rest):
        up_out, down_out, wide = rest[-3:]
        y, z, core = s[0], s[1], s[2]
        mu = mu_ref[0].astype(BF16)
        md = md_ref[0]

        first = core == 0
        for f in range(4):
            own_part, oth_part = own_ref[f], oth_ref[f]
            to = pl.multiple_of(mod4(z + f) * SUB, SUB)
            part = jnp.where(first, own_part, oth_part).reshape(3, 64, 128) * mu[f * 3 : f * 3 + 3][:, None, :]
            wide[pl.ds(to, SUB), :] = part.reshape(SUB, 128)
            part = jnp.where(first, oth_part, own_part).astype(F32).reshape(3, 64, 128)
            part = (part * md[f * 3 : f * 3 + 3][:, None, :]).reshape(SUB, 128)
            down_out[mod4(y + f), 0] = down_ref[mod4(y + f), 0] + part

        up_out[...] = up_ref[...] + wide[...].T.astype(F32)

    up_block = pl.BlockSpec((128, 4 * SUB), lambda i, s: (i, mod4(s[0] + step)))
    down_block = pl.BlockSpec((4, 1, SUB, 128), lambda i, s: (0, mod4(s[1] + step), 0, i))
    mask_block = pl.BlockSpec((1, 12, 128), lambda i, s: (step, 0, i))
    grad_block = pl.BlockSpec((4, SUB, 128), lambda i, s: (0, 0, i))
    kept = list(before)
    return call(
        f"accumulate{step}",
        body,
        (3,),
        [up_block, down_block, grad_block, grad_block, mask_block, mask_block]
        + [pl.BlockSpec(memory_space=pl.ANY)] * len(kept),
        [up_block, down_block],
        [jax.ShapeDtypeStruct(acc_up.shape, F32), jax.ShapeDtypeStruct(acc_down4.shape, F32)],
        10**7,
        6_000_000,
        aliases={7: 0, 8: 1} if kept else {},
        scratch=[pltpu.VMEM((4 * SUB, 128), BF16)],
    )(where, acc_up, acc_down4, own, oth, mask_up, mask_down, *kept)


def local(tokens, out_grad, w_up, w_down, mask_up, mask_down, acc_up, acc_down):
    row, col = lax.axis_index("row"), lax.axis_index("col")
    core, z, y = lax.rem(row, 2), lax.div(col, 4), lax.rem(col, 4)
    where = jnp.stack([y, z, core]).astype(jnp.int32)
    first = core == 0
    w_down4 = pltpu.with_memory_space_constraint(w_down.reshape(4, 4, SUB, KB), pltpu.HBM)
    w_up = pltpu.with_memory_space_constraint(w_up, pltpu.HBM)
    acc_down4 = acc_down.reshape(4, 4, SUB, KB)

    away = send("swap", jnp.where(first, out_grad, tokens), lambda x, core, z, y: (x, 1 - core, z, y))
    mine = jnp.where(first, tokens, out_grad)
    owns, oths, masks = prepare(where, w_up, w_down4, mask_up, mask_down)
    block = jnp.concatenate([jnp.where(first, mine, away), jnp.where(first, away, mine)], axis=0)
    near = [block, None, None, None]
    for step in (1, 3, 2):
        near[-step % 4] = send(f"near{step}", block, lambda x, core, z, y: merge_to(step, core, x, core, z, y))
    block_far = send("opposite", block, lambda x, core, z, y: (x + 2, core, z, y))
    *near, block_far = lax.optimization_barrier((*near, block_far))
    acts = [jnp.stack(near), None, None]
    for step in (1, 3):
        acts[(-step % 4 + 1) // 2] = send(f"tokens{step}", acts[0], lambda x, core, z, y: (x + step, core, z, y))

    weights = [[None, None] for _ in range(4)]

    def oth_to(step, value):
        weights[-step % 4][1] = send(f"w_oth{step}", value, send_weights(step, False))
        return weights[-step % 4][1]

    def own_to(step, value):
        weights[-step % 4][0] = send(f"w_own{step}", value, send_weights(step, True))
        return weights[-step % 4][0]

    owns = add_rows(where, owns, block_far)
    weights[0][0] = owns[0]
    for step in ORDER:
        oth_to(step, oths[step] if step == 2 else after(oths[step], block_far))
    for step in (1, 3, 2):
        own_to(step, owns[step])

    parts, turn = {}, where
    for step in ORDER[:3]:
        parts[step] = forward(step, turn, weights, acts)
        turn = after(where, parts[step][1])

    def to_sum(step, value, own):
        return send(f"r{step}_{int(own)}", value, send_reduce(step, own))

    half_own, half_oth = to_sum(1, parts[2][0], True), to_sum(3, parts[2][1], True)
    oth_parts = [to_sum(1, parts[1][1], False)]
    own_parts = [to_sum(3, parts[3][0], True)]
    joined_own, joined_oth = join("join_sums", where, parts[1][0], half_own, parts[3][1], half_oth)
    own_parts.append(to_sum(1, joined_own, True))
    oth_parts.append(to_sum(3, joined_oth, False))
    parts[0] = forward(0, after(turn, joined_own, joined_oth), weights, acts)
    own_parts.append(parts[0][0])
    oth_parts.append(to_sum(0, parts[0][1], False))

    own, oth = activate(where, own_parts, oth_parts)

    def to_all(step, value, is_own):
        return send(f"g{step}_{int(is_own)}", value, send_gather(step, is_own))

    left_own, right_oth = to_all(1, own, True), to_all(3, oth, False)
    cots = [
        (own, to_all(0, oth, False)),
        (to_all(3, own, True), right_oth),
        (to_all(1, left_own, True), to_all(3, right_oth, True)),
        (left_own, to_all(1, oth, False)),
    ]

    messages, totals, turn = (), {}, where
    for kind, step in PLAN:
        if kind == "w":
            messages = weight_grads(step, turn, cots[step], weights, acts, messages)
            turn = after(where, messages[0])
        else:
            totals[step] = input_grads(step, turn, cots, weights)
            turn = after(where, totals[step][0])

    ahead, behind = totals[(1, 3)]

    def to_x(step, value):
        return send(f"x{step}", value, lambda x, core, z, y: (x + step, 0, z, y) if core == 0 else None)

    def to_own(step, value):
        return send(f"d_own{step}", value, send_grads(step, True))

    def to_oth(step, value):
        return send(f"d_oth{step}", value, send_grads(step, False))

    low, high = to_x(1, totals[(2,)][0]), to_x(3, totals[(2,)][1])
    joined_low, joined_high = join("join_inputs", where, ahead, low, behind, high, SUB)
    beside = [to_x(1, joined_low), to_x(3, joined_high)]
    grads = [None] * 4
    grads[2] = (to_own(2, messages[4]), to_oth(2, messages[5]))
    (here,) = input_grads((0,), after(where, *grads[2]), cots, weights)
    grads[0] = (messages[0], to_oth(0, messages[1]))
    done = accumulate(0, where, acc_up, acc_down4, *grads[0], *masks, ())
    done = accumulate(2, where, acc_up, acc_down4, *grads[2], *masks, done)
    near_own = [to_own(step, after(messages[step * 2], *grads[2])) for step in (1, 3)]
    for step, own in zip((1, 3), near_own):
        grads[-step % 4] = (own, to_oth(step, after(messages[step * 2 + 1], *grads[2])))
    sums = [after(here, *near_own, *done), *beside]
    part = sum(s.astype(F32) for s in sums).astype(BF16)
    pieces = [part[:, :KB]]
    for step in (1, 2, 3):
        pieces.append(
            send(
                f"y{step}",
                part[:, step * KB : (step + 1) * KB],
                lambda x, core, z, y: (x, 0, z, y + step) if core == 0 else None,
            )
        )
    done = accumulate(3, where, acc_up, acc_down4, *grads[3], *masks, done)
    pieces[0] = after(pieces[0], done[0])
    both = sum(p.astype(F32) for p in pieces).astype(BF16)
    other = send("hand_over", both[SUB:], lambda x, core, z, y: (x, 1, z, y) if core == 0 else None)
    in_grad = jnp.where(first, both[:SUB], other)
    done = accumulate(1, where, acc_up, acc_down4, *grads[1], *masks, done)
    return (in_grad, done[0], done[1].reshape(acc_down.shape))


def solution(mesh):
    placed = (
        P("row", "col"),
        P("row", "col"),
        P("col", "row"),
        P("row", "col"),
        P("col", "row"),
        P("row", "col"),
        P("col", "row"),
        P("row", "col"),
    )
    return jax.shard_map(
        local,
        mesh=mesh,
        in_specs=placed,
        out_specs=(P("row", "col"), P("col", "row"), P("row", "col")),
        check_vma=False,
    )
```
